512 devices in a mesh: gx: 16 (over z, y_hi), gy: 8 (over y_lo, core), gz: 4 (over x).
Axes of the slice: x: 4, y: 8 (y_hi: 2, y_lo: 4; y = y_hi * 4 + y_lo), z: 8, core: 2. Of those that a mesh axis runs over, the one named last changes fastest.
Arguments:
- populations: float32 [19, 16, 128, 4096], P(None, None, ('gy', 'gz'), 'gx'), may hold values from 0 to 0.5, as said below
- cell_type: int32 [16, 128, 4096], P(None, ('gy', 'gz'), 'gx'), may hold values from 0 to 2, as said below
- adjoint: float32 [7, 16, 128, 4096], P(None, 'gz', 'gy', 'gx'), may hold values from -6 to 6
Outputs:
- flow_next: float32 [19, 16, 128, 4096], P(None, None, ('gy', 'gz'), 'gx')
- adjoint_prev: float32 [7, 16, 128, 4096], P(None, 'gz', 'gy', 'gx')
The draws below stay inside these ranges and needn't reach their ends.
Inputs may be any that keep to these rules, and one draw needn't show every extreme that they name: `cell_type`: layers below 8 are solid (code 1), with code 2 cells only in layer 0; layers from 8 on hold codes 0 and 1, and a cell's code is the same in all of them. `populations`: each population is its lattice weight times a positive factor near one.
All inputs are finite; a program needn't handle non-finite values.
Results may differ from the reference program's by a relative error of at most 0.000065.
Values sent between devices are 32-bit elements; how exact they have to be, the bound alone decides.
No kernel may reach another device: no remote copies, remote signals or barrier semaphores. Data moves between devices by JAX's collectives and lax.ppermute only.
A program may use at most 64 MiB of HBM per device.

```python
import jax
import jax.numpy as jnp
from jax import lax

BASE = 8
DEPTH = 16
ROWS = 128
CELLS_X = 4096


WEIGHT_TABLE = [1.0 / 3.0] + [1.0 / 18.0] * 6 + [1.0 / 36.0] * 12


DRIFT_TABLE = [1.0, 1.1, 0.9, 1.0, 1.0, 1.0, 1.0, 1.1, 0.9, 1.1, 0.9, 1.1, 0.9, 1.1, 0.9, 1.0, 1.0, 1.0, 1.0]


def draw_populations(key, part):
    shape = (19, DEPTH, ROWS, CELLS_X)
    factor = 1.0 + 0.1 * jax.random.truncated_normal(key, -2.5, 2.5, shape, jnp.float32)
    scale = jnp.array(WEIGHT_TABLE, jnp.float32) * jnp.array(DRIFT_TABLE, jnp.float32)
    return scale[:, None, None, None] * factor


def draw_cell_type(key, part):
    key_pin, key_heat = jax.random.split(jax.random.fold_in(key, 11))
    pillar = jax.random.randint(key_pin, (ROWS, CELLS_X), 0, 10) < 3
    heated = jax.random.randint(key_heat, (ROWS, CELLS_X), 0, 4) == 0
    layer = jnp.arange(DEPTH)[:, None, None]
    base = jnp.where((layer == 0) & heated[None], 2, 1)
    upper = jnp.where(pillar[None], 1, 0)
    return jnp.where(layer < BASE, base, upper).astype(jnp.int32)


def level_of(stream_key, extent, shards, low, top_value):
    level, own = 1.0, jax.random.fold_in(stream_key, 6)
    for axis_at, parts in shards:
        draws = jnp.exp(jax.random.uniform(jax.random.fold_in(own, axis_at), (parts,), jnp.float32, low / len(shards), top_value / len(shards)))
        level = level * jnp.repeat(draws, extent[axis_at] // parts).reshape([-1 if axis == axis_at else 1 for axis in range(len(extent))])
    return level


def noise(key, dims, deviation, most, shards=(), held_as=jnp.bfloat16):
    entries = jax.random.normal(key, dims, jnp.float32) * deviation
    if len(shards) > 0:
        entries = level_of(key, dims, shards, -0.22, 0.18) * entries
    return jnp.clip(entries, min=-most, max=most).astype(held_as)


def setup_inputs(seed: int = 0) -> dict:
    streams_of = jax.random.split(jax.random.key(seed), 4)
    populations = draw_populations(jax.random.fold_in(streams_of[3], 71), 0)
    cell_type = draw_cell_type(jax.random.fold_in(streams_of[3], 71), 0)
    adjoint = noise(streams_of[2], (7, DEPTH, ROWS, CELLS_X), 1.0, 6.0, ((1, 4), (2, 8), (3, 16)), jnp.float32)
    return {"populations": populations, "cell_type": cell_type, "adjoint": adjoint}


VEL19 = [(0, 0, 0), (1, 0, 0), (-1, 0, 0), (0, 1, 0), (0, -1, 0), (0, 0, 1), (0, 0, -1),
         (1, 1, 0), (-1, -1, 0), (1, -1, 0), (-1, 1, 0), (1, 0, 1), (-1, 0, -1), (1, 0, -1), (-1, 0, 1),
         (0, 1, 1), (0, -1, -1), (0, 1, -1), (0, -1, 1)]
WEIGHT19 = [1.0 / 3.0] + [1.0 / 18.0] * 6 + [1.0 / 36.0] * 12
OPPOSITE = [0, 2, 1, 4, 3, 6, 5, 8, 7, 10, 9, 12, 11, 14, 13, 16, 15, 18, 17]
VEL7 = [(0, 0, 0), (1, 0, 0), (-1, 0, 0), (0, 1, 0), (0, -1, 0), (0, 0, 1), (0, 0, -1)]
WEIGHT7 = [0.25] + [0.125] * 6
OMEGA_FLOW = 1.6
OMEGA_FLUID = 1.25
OMEGA_SOLID = 1.6


def moments(pops):
    table = jnp.array(VEL19, jnp.float32).T
    density = jnp.sum(pops, axis=0)
    momentum = jnp.tensordot(table, pops, axes=1, precision=lax.Precision.HIGHEST)
    return density, momentum / density


def collide(pops):
    density, velocity = moments(pops)
    usq = jnp.sum(velocity * velocity, axis=0)
    outs = []
    for i in range(19):
        cx, cy, cz = VEL19[i]
        cu = cx * velocity[0] + cy * velocity[1] + cz * velocity[2]
        feq = WEIGHT19[i] * density * (1.0 + 3.0 * cu + 4.5 * cu * cu - 1.5 * usq)
        outs.append(pops[i] - OMEGA_FLOW * (pops[i] - feq))
    return jnp.stack(outs)


def stream(padded, post, pops, fluid):
    depth, rows, cols = fluid.shape
    outs = []
    for i in range(19):
        cx, cy, cz = VEL19[i]
        src = padded[i, 1 - cz:1 - cz + depth, 1 - cy:1 - cy + rows, 1 - cx:1 - cx + cols]
        flag = padded[19, 1 - cz:1 - cz + depth, 1 - cy:1 - cy + rows, 1 - cx:1 - cx + cols]
        pulled = flag * src + (1.0 - flag) * post[OPPOSITE[i]]
        outs.append(jnp.where(fluid > 0.5, pulled, pops[i]))
    return jnp.stack(outs)


def thermal(padded, velocity, codes):
    depth, rows, cols = codes.shape
    pulled = []
    for j in range(7):
        ex, ey, ez = VEL7[j]
        pulled.append(padded[j, 1 + ez:1 + ez + depth, 1 + ey:1 + ey + rows, 1 + ex:1 + ex + cols])
    mean_term = sum(WEIGHT7[j] * pulled[j] for j in range(7))
    flux = [sum(WEIGHT7[j] * VEL7[j][k] * pulled[j] for j in range(7)) for k in range(3)]
    coupled = mean_term + 4.0 * (velocity[0] * flux[0] + velocity[1] * flux[1] + velocity[2] * flux[2])
    omega = jnp.where(codes == 0.0, OMEGA_FLUID, OMEGA_SOLID)
    source = jnp.where(codes == 2.0, 1.0, 0.0)
    return jnp.stack([(1.0 - omega) * pulled[j] + omega * coupled + source for j in range(7)])


def reference(populations, cell_type, adjoint):
    fluid = jnp.where(cell_type == 0, 1.0, 0.0).astype(jnp.float32)
    post = collide(populations)
    stacked = jnp.concatenate([post, fluid[None]], axis=0)
    padded = jnp.pad(stacked, ((0, 0), (1, 1), (1, 1), (1, 1)))
    flow_next = stream(padded, post, populations, fluid)
    density = jnp.sum(flow_next, axis=0)
    table = jnp.array(VEL19, jnp.float32).T
    velocity = jnp.tensordot(table, flow_next, axes=1, precision=lax.Precision.HIGHEST) / density * fluid
    codes = cell_type.astype(jnp.float32)
    heat_pad = jnp.pad(adjoint, ((0, 0), (1, 1), (1, 1), (1, 1)))
    adjoint_prev = thermal(heat_pad, velocity, codes)
    return flow_next, adjoint_prev
```

```python
import jax
import jax.numpy as jnp
from jax import lax
from jax.experimental import pallas as pl
from jax.experimental.pallas import tpu as pltpu
from jax.sharding import PartitionSpec as P

VEL19 = [
    (0, 0, 0),
    (1, 0, 0),
    (-1, 0, 0),
    (0, 1, 0),
    (0, -1, 0),
    (0, 0, 1),
    (0, 0, -1),
    (1, 1, 0),
    (-1, -1, 0),
    (1, -1, 0),
    (-1, 1, 0),
    (1, 0, 1),
    (-1, 0, -1),
    (1, 0, -1),
    (-1, 0, 1),
    (0, 1, 1),
    (0, -1, -1),
    (0, 1, -1),
    (0, -1, 1),
]
WEIGHT19 = [1.0 / 3.0] + [1.0 / 18.0] * 6 + [1.0 / 36.0] * 12
OPPOSITE = [0, 2, 1, 4, 3, 6, 5, 8, 7, 10, 9, 12, 11, 14, 13, 16, 15, 18, 17]
WEIGHT7 = [0.25] + [0.125] * 6
OMEGA_FLOW = 1.6
OMEGA_FLUID = 1.25
OMEGA_SOLID = 1.6

BASE = 8
TOP = 8
LANES = 128
XP = [1, 7, 9, 11, 13]
XM = [2, 8, 10, 12, 14]
YP = [3, 7, 10, 15, 17]
YM = [4, 8, 9, 16, 18]
YALL = YP + YM
FLAG_LANE = 40
HEAT_LANE = 64
FLAG_ROW = 40
CORNER_ROW = 41
HEAT_ROW = 48
Y_ROWS = 64
VMEM = pl.BlockSpec(memory_space=pltpu.VMEM)


def f32(*shape):
    return jax.ShapeDtypeStruct(shape, jnp.float32)


def iota(shape, axis):
    return lax.broadcasted_iota(jnp.int32, shape, axis)


def roll(value, shift, axis=1):
    size = value.shape[axis]
    shift = shift % size
    return value if shift == 0 else pltpu.roll(value, shift, axis)


def collide_kernel(pops, cells, adj, post, ysh, xp, xm, yp, ym, gp, gm):
    rows, cols = cells.shape[1:]
    left, right = slice(0, LANES), slice(cols - LANES, cols)
    lane = iota((rows, LANES), 1)
    fluid = jnp.where(cells[BASE] == 0, 1.0, 0.0)
    to_right = jnp.where(lane == FLAG_LANE, roll(fluid[:, right], FLAG_LANE + 1), 0.0)
    to_left = jnp.where(lane == FLAG_LANE, roll(fluid[:, left], FLAG_LANE), 0.0)
    yp[FLAG_ROW : FLAG_ROW + 1, :] = fluid[rows - 1 : rows]
    ym[FLAG_ROW : FLAG_ROW + 1, :] = fluid[0:1]
    for level in range(TOP):
        f = [pops[i, BASE + level] for i in range(19)]
        density = sum(f[1:], f[0])
        u = []
        for k in range(3):
            plus = sum(f[i] for i in range(19) if VEL19[i][k] == 1)
            minus = sum(f[i] for i in range(19) if VEL19[i][k] == -1)
            u.append((plus - minus) / density)
        common = 1.0 - 1.5 * (u[0] * u[0] + u[1] * u[1] + u[2] * u[2])
        scaled = OMEGA_FLOW * density
        for i in range(19):
            c = VEL19[i]
            cu = None
            for k in range(3):
                if c[k]:
                    term = u[k] if c[k] == 1 else -u[k]
                    cu = term if cu is None else cu + term
            shape = common if cu is None else common + cu * (3.0 + 4.5 * cu)
            out = (1.0 - OMEGA_FLOW) * f[i] + (WEIGHT19[i] * scaled) * shape
            post[i, level] = out
            if i in XP:
                at = XP.index(i) * TOP + level
                to_right = jnp.where(lane == at, roll(out[:, right], at + 1), to_right)
            if i in XM:
                at = XM.index(i) * TOP + level
                to_left = jnp.where(lane == at, roll(out[:, left], at), to_left)
            if i in YP:
                at = YP.index(i) * TOP + level
                yp[at : at + 1, :] = out[rows - 1 : rows]
                ysh[YALL.index(i), level, 1:rows, :] = out[0 : rows - 1]
            if i in YM:
                at = YM.index(i) * TOP + level
                ym[at : at + 1, :] = out[0:1]
                ysh[YALL.index(i), level, 0 : rows - 1, :] = out[1:rows]
    layers, arows = adj.shape[1:3]
    lane = iota((arows, LANES), 1)
    heat_right = jnp.zeros((arows, LANES), jnp.float32)
    heat_left = heat_right
    for z in range(layers):
        at = HEAT_LANE + z
        heat_right = jnp.where(lane == at, roll(adj[2, z, :, right], at + 1), heat_right)
        heat_left = jnp.where(lane == at, roll(adj[1, z, :, left], at), heat_left)
        gp[z : z + 1, :] = adj[4, z, arows - 1 : arows, :]
        gm[z : z + 1, :] = adj[3, z, 0:1, :]
    xp[...] = heat_right
    xm[...] = heat_left
    lane = iota((rows, LANES), 1)
    xp[0:rows, :] = jnp.where(lane < HEAT_LANE, to_right, heat_right[0:rows])
    xm[0:rows, :] = jnp.where(lane < HEAT_LANE, to_left, heat_left[0:rows])
    yp[HEAT_ROW : HEAT_ROW + arows, :] = adj[6, layers - 1]
    ym[HEAT_ROW : HEAT_ROW + arows, :] = adj[5, 0]


def stream_kernel(post, ysh, pops, cells, xl, xr, yu, yd, out, vel, ext):
    rows, cols = cells.shape[1:]
    last = cols - LANES
    sub = iota((rows, cols), 0)
    col = iota((rows, LANES), 1)

    ext[0, 0:1, :] = yu[CORNER_ROW : CORNER_ROW + 1, 0:LANES]
    ext[1, 0:1, :] = yu[CORNER_ROW : CORNER_ROW + 1, LANES : 2 * LANES]
    ext[0, 1 : rows + 1, :] = xl[0:rows, :]
    ext[1, 1 : rows + 1, :] = xr[0:rows, :]
    ext[0, rows + 1 : rows + 2, :] = yd[CORNER_ROW : CORNER_ROW + 1, 0:LANES]
    ext[1, rows + 1 : rows + 2, :] = yd[CORNER_ROW : CORNER_ROW + 1, LANES : 2 * LANES]
    beyond = {
        (side, cy): ext[side, 1 - cy : 1 - cy + rows, :] for side in (0, 1) for cy in (-1, 0, 1)
    }

    def shift_x(value, cx, cy, lane_at):
        if cx == 0:
            return value
        value = roll(value, cx)
        if cx == 1:
            edge = roll(beyond[0, cy], -lane_at)
            patched = jnp.where(col == 0, edge, value[:, 0:LANES])
            return jnp.concatenate([patched, value[:, LANES:]], axis=1)
        edge = roll(beyond[1, cy], LANES - 1 - lane_at)
        patched = jnp.where(col == LANES - 1, edge, value[:, last:])
        return jnp.concatenate([value[:, 0:last], patched], axis=1)

    def shift_y(value, cy, halo):
        if cy == 0:
            return value
        halo = jnp.broadcast_to(halo, (rows, cols))
        return jnp.where(sub == (0 if cy == 1 else rows - 1), halo, value)

    fluid = jnp.where(cells[BASE] == 0, 1.0, 0.0)
    is_fluid = fluid > 0.5
    spread = {0: fluid}
    spread[1] = shift_y(
        jnp.concatenate([fluid[rows - 1 : rows], fluid[0 : rows - 1]], axis=0),
        1,
        yu[FLAG_ROW : FLAG_ROW + 1, :],
    )
    spread[-1] = shift_y(
        jnp.concatenate([fluid[1:rows], fluid[0:1]], axis=0), -1, yd[FLAG_ROW : FLAG_ROW + 1, :]
    )
    open_from = {
        (cx, cy): shift_x(spread[cy], cx, cy, FLAG_LANE) > 0.5
        for cx in (-1, 0, 1)
        for cy in (-1, 0, 1)
    }

    out[:, 0:BASE] = pops[:, 0:BASE]
    vel[0] = jnp.zeros(vel.shape[1:], jnp.float32)
    vel[1] = jnp.zeros(vel.shape[1:], jnp.float32)
    layers = (vel.shape[1] - 1) // 3
    vel[0, 3 * layers] = jnp.where(cells[0] == 2, 1.0, 0.0)
    vel[2, 3 * layers] = fluid
    vel[3, 3 * layers] = fluid
    for level in range(TOP):
        density = None
        momentum = [None, None, None]
        for i in range(19):
            cx, cy, cz = VEL19[i]
            before = pops[i, BASE + level]
            back = post[OPPOSITE[i], level]
            source = level - cz
            if i == 0:
                pulled = back
            elif source < 0 or source >= TOP:
                pulled = back
            else:
                if cy == 0:
                    value = post[i, source]
                else:
                    at = (YP if cy == 1 else YM).index(i) * TOP + source
                    halo = (yu if cy == 1 else yd)[at : at + 1, :]
                    value = shift_y(ysh[YALL.index(i), source], cy, halo)
                if cx:
                    value = shift_x(value, cx, cy, (XP if cx == 1 else XM).index(i) * TOP + source)
                pulled = jnp.where(open_from[cx, cy], value, back)
            new = jnp.where(is_fluid, pulled, before)
            out[i, BASE + level] = new
            density = new if density is None else density + new
            for k in range(3):
                c = VEL19[i][k]
                if c:
                    term = new if c == 1 else -new
                    momentum[k] = term if momentum[k] is None else momentum[k] + term
        for k in range(3):
            vel[2 + level // layers, k * layers + level % layers] = jnp.where(
                is_fluid, momentum[k] / density, 0.0
            )


def thermal_kernel(where_z, adj, va, xl, xr, yu, yd, gu, gd, out, wide):
    layers, rows, cols = adj.shape[1:]
    gz, shards = where_z[0], where_z[1]
    srcs, planes, part = va.shape[:3]
    last = cols - LANES
    for q in range(planes):
        for s in range(srcs):
            wide[q, part * s : part * (s + 1), :] = va[s, q]
    sub = iota((rows, cols), 0)
    col = iota((rows, LANES), 1)
    mark = wide[planes - 1]
    is_fluid = (mark * jnp.where(gz >= shards // 2, 1.0, 0.0)) > 0.5
    heated = mark * jnp.where(gz == 0, 1.0, 0.0)
    below = jnp.where(gz == 0, 0.0, yu[HEAT_ROW : HEAT_ROW + rows, :])
    above = jnp.where(gz == shards - 1, 0.0, yd[HEAT_ROW : HEAT_ROW + rows, :])
    omega = jnp.where(is_fluid, OMEGA_FLUID, OMEGA_SOLID)
    for z in range(layers):
        p = [adj[0, z]]
        ahead = roll(adj[1, z], -1)
        edge = roll(xr[...], LANES - 1 - (HEAT_LANE + z))
        p.append(
            jnp.concatenate(
                [ahead[:, 0:last], jnp.where(col == LANES - 1, edge, ahead[:, last:])], axis=1
            )
        )
        behind = roll(adj[2, z], 1)
        edge = roll(xl[...], -(HEAT_LANE + z))
        p.append(
            jnp.concatenate(
                [jnp.where(col == 0, edge, behind[:, 0:LANES]), behind[:, LANES:]], axis=1
            )
        )
        halo = jnp.broadcast_to(gd[z : z + 1, :], (rows, cols))
        p.append(jnp.where(sub == rows - 1, halo, roll(adj[3, z], -1, 0)))
        halo = jnp.broadcast_to(gu[z : z + 1, :], (rows, cols))
        p.append(jnp.where(sub == 0, halo, roll(adj[4, z], 1, 0)))
        p.append(adj[5, z + 1] if z + 1 < layers else above)
        p.append(adj[6, z - 1] if z > 0 else below)
        mean = WEIGHT7[0] * p[0] + WEIGHT7[1] * (p[1] + p[2] + p[3] + p[4] + p[5] + p[6])
        dot = (
            wide[z] * (p[1] - p[2])
            + wide[layers + z] * (p[3] - p[4])
            + wide[2 * layers + z] * (p[5] - p[6])
        )
        common = omega * (mean + 4.0 * WEIGHT7[1] * dot)
        if z == 0:
            common = common + heated
        for j in range(7):
            out[j, z] = (1.0 - omega) * p[j] + common


def per_device(populations, cell_type, adjoint, sizes):
    nx, ny, nz = sizes
    axes = ("gx", "gy", "gz")

    def along(delta_x, delta_y):
        moves = []
        for a in range(nx):
            for b in range(ny * nz):
                a2, b2 = a + delta_x, b + delta_y
                if 0 <= a2 < nx and 0 <= b2 < ny * nz:
                    moves.append((a * ny * nz + b, a2 * ny * nz + b2))
        return moves

    def across(delta):
        moves = []
        for a in range(nx):
            for b in range(ny):
                for c in range(nz):
                    if 0 <= b + delta < ny:
                        moves.append(((a * ny + b) * nz + c, (a * ny + b + delta) * nz + c))
        return moves

    depth, rows, cols = cell_type.shape
    layers, heat_rows = adjoint.shape[1:3]
    post, ysh, xp, xm, yp, ym, gp, gm = pl.pallas_call(
        collide_kernel,
        out_shape=(
            f32(19, TOP, rows, cols),
            f32(10, TOP, rows, cols),
            f32(heat_rows, LANES),
            f32(heat_rows, LANES),
            f32(Y_ROWS, cols),
            f32(Y_ROWS, cols),
            f32(layers, cols),
            f32(layers, cols),
        ),
        in_specs=[VMEM] * 3,
        out_specs=(VMEM,) * 8,
        name="collide",
    )(populations, cell_type, adjoint)
    xl = lax.ppermute(xp, axes, along(1, 0))
    xr = lax.ppermute(xm, axes, along(-1, 0))
    gu = lax.ppermute(gp, axes, across(1))
    gd = lax.ppermute(gm, axes, across(-1))
    top = jnp.concatenate([xl[rows - 1 : rows], xr[rows - 1 : rows]], axis=1)
    bottom = jnp.concatenate([xl[0:1], xr[0:1]], axis=1)
    yp = lax.dynamic_update_slice(yp, top, (CORNER_ROW, 0))
    ym = lax.dynamic_update_slice(ym, bottom, (CORNER_ROW, 0))
    yu = lax.ppermute(yp, axes, along(0, 1))
    yd = lax.ppermute(ym, axes, along(0, -1))
    flow_next, vel = pl.pallas_call(
        stream_kernel,
        out_shape=(f32(*populations.shape), f32(nz, 3 * layers + 1, rows, cols)),
        in_specs=[VMEM] * 8,
        out_specs=(VMEM,) * 2,
        scratch_shapes=[pltpu.VMEM((2, 8, LANES), jnp.float32)],
        name="stream",
    )(post, ysh, populations, cell_type, xl, xr, yu, yd)
    va = lax.all_to_all(vel, "gz", split_axis=0, concat_axis=0, tiled=True)
    where_z = jnp.stack([lax.axis_index("gz"), jnp.int32(nz)])
    adjoint_prev = pl.pallas_call(
        thermal_kernel,
        out_shape=f32(*adjoint.shape),
        in_specs=[pl.BlockSpec(memory_space=pltpu.SMEM)] + [VMEM] * 8,
        out_specs=VMEM,
        scratch_shapes=[pltpu.VMEM((3 * layers + 1, heat_rows, cols), jnp.float32)],
        name="thermal",
    )(where_z, adjoint, va, xl, xr, yu, yd, gu, gd)
    return flow_next, adjoint_prev


def solution(mesh):
    sizes = tuple(mesh.shape[axis] for axis in ("gx", "gy", "gz"))
    placed = (
        P(None, None, ("gy", "gz"), "gx"),
        P(None, ("gy", "gz"), "gx"),
        P(None, "gz", "gy", "gx"),
    )
    return jax.shard_map(
        lambda p, c, a: per_device(p, c, a, sizes),
        mesh=mesh,
        in_specs=placed,
        out_specs=(P(None, None, ("gy", "gz"), "gx"), P(None, "gz", "gy", "gx")),
        check_vma=False,
    )
```

```python
import functools

import jax
import jax.numpy as jnp
from jax import lax
from jax.experimental import pallas as pl
from jax.experimental.pallas import tpu as pltpu
from jax.sharding import PartitionSpec as P


VEL19 = [
    (0, 0, 0),
    (1, 0, 0),
    (-1, 0, 0),
    (0, 1, 0),
    (0, -1, 0),
    (0, 0, 1),
    (0, 0, -1),
    (1, 1, 0),
    (-1, -1, 0),
    (1, -1, 0),
    (-1, 1, 0),
    (1, 0, 1),
    (-1, 0, -1),
    (1, 0, -1),
    (-1, 0, 1),
    (0, 1, 1),
    (0, -1, -1),
    (0, 1, -1),
    (0, -1, 1),
]
WEIGHT19 = [1.0 / 3.0] + [1.0 / 18.0] * 6 + [1.0 / 36.0] * 12
OPPOSITE = [0, 2, 1, 4, 3, 6, 5, 8, 7, 10, 9, 12, 11, 14, 13, 16, 15, 18, 17]
WEIGHT7 = [0.25] + [0.125] * 6
OMEGA_FLOW = 1.6
OMEGA_FLUID = 1.25
OMEGA_SOLID = 1.6

BASE = 8
TOP = 8
LANES = 128
XP = [1, 7, 9, 11, 13]
XM = [2, 8, 10, 12, 14]
YP = [3, 7, 10, 15, 17]
YM = [4, 8, 9, 16, 18]
YALL = YP + YM
FLAG_LANE = 40
HEAT_LANE = 64
FLAG_ROW = 40
CORNER_ROW = 41
HEAT_ROW = 48
Y_ROWS = 64
VMEM = pl.BlockSpec(memory_space=pltpu.VMEM)


def f32(*shape):
    return jax.ShapeDtypeStruct(shape, jnp.float32)


def iota(shape, axis):
    return lax.broadcasted_iota(jnp.int32, shape, axis)


def roll(value, shift, axis=1):
    size = value.shape[axis]
    shift = shift % size
    return value if shift == 0 else pltpu.roll(value, shift, axis)


def collide_kernel(
    pops_in, cells_in, adj_in, post, ysh, xp, xm, yp, ym, gp, gm, pops, cells, adj, sem
):
    rows, cols = cells.shape[1:]
    half = TOP // 2
    loads = [
        pltpu.make_async_copy(cells_in.at[BASE], cells.at[0], sem.at[0]),
        pltpu.make_async_copy(
            pops_in.at[:, BASE : BASE + half], pops.at[:, 0:half], sem.at[1]
        ),
        pltpu.make_async_copy(
            pops_in.at[:, BASE + half : BASE + TOP], pops.at[:, half:TOP], sem.at[2]
        ),
        pltpu.make_async_copy(adj_in, adj, sem.at[3]),
    ]
    for load in loads:
        load.start()
    loads[0].wait()
    left, right = slice(0, LANES), slice(cols - LANES, cols)
    lane = iota((rows, LANES), 1)
    fluid = jnp.where(cells[0] == 0, 1.0, 0.0)
    to_right = jnp.where(lane == FLAG_LANE, roll(fluid[:, right], FLAG_LANE + 1), 0.0)
    to_left = jnp.where(lane == FLAG_LANE, roll(fluid[:, left], FLAG_LANE), 0.0)
    yp[FLAG_ROW : FLAG_ROW + 1, :] = fluid[rows - 1 : rows]
    ym[FLAG_ROW : FLAG_ROW + 1, :] = fluid[0:1]
    for level in range(TOP):
        if level % half == 0:
            loads[1 + level // half].wait()
        f = [pops[i, level] for i in range(19)]
        density = sum(f[1:], f[0])
        u = []
        for k in range(3):
            plus = sum(f[i] for i in range(19) if VEL19[i][k] == 1)
            minus = sum(f[i] for i in range(19) if VEL19[i][k] == -1)
            u.append((plus - minus) / density)
        common = 1.0 - 1.5 * (u[0] * u[0] + u[1] * u[1] + u[2] * u[2])
        scaled = OMEGA_FLOW * density
        for i in range(19):
            c = VEL19[i]
            cu = None
            for k in range(3):
                if c[k]:
                    term = u[k] if c[k] == 1 else -u[k]
                    cu = term if cu is None else cu + term
            shape = common if cu is None else common + cu * (3.0 + 4.5 * cu)
            out = (1.0 - OMEGA_FLOW) * f[i] + (WEIGHT19[i] * scaled) * shape
            post[i, level] = out
            if i in XP:
                at = XP.index(i) * TOP + level
                to_right = jnp.where(lane == at, roll(out[:, right], at + 1), to_right)
            if i in XM:
                at = XM.index(i) * TOP + level
                to_left = jnp.where(lane == at, roll(out[:, left], at), to_left)
            if i in YP:
                at = YP.index(i) * TOP + level
                yp[at : at + 1, :] = out[rows - 1 : rows]
                ysh[YALL.index(i), level, 1:rows, :] = out[0 : rows - 1]
            if i in YM:
                at = YM.index(i) * TOP + level
                ym[at : at + 1, :] = out[0:1]
                ysh[YALL.index(i), level, 0 : rows - 1, :] = out[1:rows]
    loads[3].wait()
    layers, arows = adj.shape[1:3]
    lane = iota((arows, LANES), 1)
    heat_right = jnp.zeros((arows, LANES), jnp.float32)
    heat_left = heat_right
    for z in range(layers):
        at = HEAT_LANE + z
        heat_right = jnp.where(lane == at, roll(adj[2, z, :, right], at + 1), heat_right)
        heat_left = jnp.where(lane == at, roll(adj[1, z, :, left], at), heat_left)
        gp[z : z + 1, :] = adj[4, z, arows - 1 : arows, :]
        gm[z : z + 1, :] = adj[3, z, 0:1, :]
    xp[...] = heat_right
    xm[...] = heat_left
    lane = iota((rows, LANES), 1)
    xp[0:rows, :] = jnp.where(lane < HEAT_LANE, to_right, heat_right[0:rows])
    xm[0:rows, :] = jnp.where(lane < HEAT_LANE, to_left, heat_left[0:rows])
    yp[HEAT_ROW : HEAT_ROW + arows, :] = adj[6, layers - 1]
    ym[HEAT_ROW : HEAT_ROW + arows, :] = adj[5, 0]


def stream_kernel(post, ysh, pops, cells, xl, xr, yu, yd, out, vel, ext):
    rows, cols = cells.shape[1:]
    last = cols - LANES
    sub = iota((rows, cols), 0)
    col = iota((rows, LANES), 1)

    ext[0, 0:1, :] = yu[CORNER_ROW : CORNER_ROW + 1, 0:LANES]
    ext[1, 0:1, :] = yu[CORNER_ROW : CORNER_ROW + 1, LANES : 2 * LANES]
    ext[0, 1 : rows + 1, :] = xl[0:rows, :]
    ext[1, 1 : rows + 1, :] = xr[0:rows, :]
    ext[0, rows + 1 : rows + 2, :] = yd[CORNER_ROW : CORNER_ROW + 1, 0:LANES]
    ext[1, rows + 1 : rows + 2, :] = yd[CORNER_ROW : CORNER_ROW + 1, LANES : 2 * LANES]
    beyond = {
        (side, cy): ext[side, 1 - cy : 1 - cy + rows, :] for side in (0, 1) for cy in (-1, 0, 1)
    }

    def shift_x(value, cx, cy, lane_at):
        if cx == 0:
            return value
        value = roll(value, cx)
        if cx == 1:
            edge = roll(beyond[0, cy], -lane_at)
            patched = jnp.where(col == 0, edge, value[:, 0:LANES])
            return jnp.concatenate([patched, value[:, LANES:]], axis=1)
        edge = roll(beyond[1, cy], LANES - 1 - lane_at)
        patched = jnp.where(col == LANES - 1, edge, value[:, last:])
        return jnp.concatenate([value[:, 0:last], patched], axis=1)

    def shift_y(value, cy, halo):
        if cy == 0:
            return value
        halo = jnp.broadcast_to(halo, (rows, cols))
        return jnp.where(sub == (0 if cy == 1 else rows - 1), halo, value)

    fluid = jnp.where(cells[BASE] == 0, 1.0, 0.0)
    is_fluid = fluid > 0.5
    spread = {0: fluid}
    spread[1] = shift_y(
        jnp.concatenate([fluid[rows - 1 : rows], fluid[0 : rows - 1]], axis=0),
        1,
        yu[FLAG_ROW : FLAG_ROW + 1, :],
    )
    spread[-1] = shift_y(
        jnp.concatenate([fluid[1:rows], fluid[0:1]], axis=0), -1, yd[FLAG_ROW : FLAG_ROW + 1, :]
    )
    open_from = {
        (cx, cy): shift_x(spread[cy], cx, cy, FLAG_LANE) > 0.5
        for cx in (-1, 0, 1)
        for cy in (-1, 0, 1)
    }

    out[:, 0:BASE] = pops[:, 0:BASE]
    vel[0] = jnp.zeros(vel.shape[1:], jnp.float32)
    vel[1] = jnp.zeros(vel.shape[1:], jnp.float32)
    layers = (vel.shape[1] - 1) // 3
    vel[0, 3 * layers] = jnp.where(cells[0] == 2, 1.0, 0.0)
    vel[2, 3 * layers] = fluid
    vel[3, 3 * layers] = fluid
    for level in range(TOP):
        density = None
        momentum = [None, None, None]
        for i in range(19):
            cx, cy, cz = VEL19[i]
            before = pops[i, BASE + level]
            back = post[OPPOSITE[i], level]
            source = level - cz
            if i == 0:
                pulled = back
            elif source < 0 or source >= TOP:
                pulled = back
            else:
                if cy == 0:
                    value = post[i, source]
                else:
                    at = (YP if cy == 1 else YM).index(i) * TOP + source
                    halo = (yu if cy == 1 else yd)[at : at + 1, :]
                    value = shift_y(ysh[YALL.index(i), source], cy, halo)
                if cx:
                    value = shift_x(value, cx, cy, (XP if cx == 1 else XM).index(i) * TOP + source)
                pulled = jnp.where(open_from[cx, cy], value, back)
            new = jnp.where(is_fluid, pulled, before)
            out[i, BASE + level] = new
            density = new if density is None else density + new
            for k in range(3):
                c = VEL19[i][k]
                if c:
                    term = new if c == 1 else -new
                    momentum[k] = term if momentum[k] is None else momentum[k] + term
        for k in range(3):
            vel[2 + level // layers, k * layers + level % layers] = jnp.where(
                is_fluid, momentum[k] / density, 0.0
            )


def thermal_kernel(shards, adj, va, xl, xr, yu, yd, gu, gd, out, wide):
    layers, rows, cols = adj.shape[1:]
    gz = lax.axis_index("gz")
    srcs, planes, part = va.shape[:3]
    last = cols - LANES
    for q in range(planes):
        for s in range(srcs):
            wide[q, part * s : part * (s + 1), :] = va[s, q]
    sub = iota((rows, cols), 0)
    col = iota((rows, LANES), 1)
    mark = wide[planes - 1]
    is_fluid = (mark * jnp.where(gz >= shards // 2, 1.0, 0.0)) > 0.5
    heated = mark * jnp.where(gz == 0, 1.0, 0.0)
    below = jnp.where(gz == 0, 0.0, yu[HEAT_ROW : HEAT_ROW + rows, :])
    above = jnp.where(gz == shards - 1, 0.0, yd[HEAT_ROW : HEAT_ROW + rows, :])
    omega = jnp.where(is_fluid, OMEGA_FLUID, OMEGA_SOLID)
    for z in range(layers):
        p = [adj[0, z]]
        ahead = roll(adj[1, z], -1)
        edge = roll(xr[...], LANES - 1 - (HEAT_LANE + z))
        p.append(
            jnp.concatenate(
                [ahead[:, 0:last], jnp.where(col == LANES - 1, edge, ahead[:, last:])], axis=1
            )
        )
        behind = roll(adj[2, z], 1)
        edge = roll(xl[...], -(HEAT_LANE + z))
        p.append(
            jnp.concatenate(
                [jnp.where(col == 0, edge, behind[:, 0:LANES]), behind[:, LANES:]], axis=1
            )
        )
        halo = jnp.broadcast_to(gd[z : z + 1, :], (rows, cols))
        p.append(jnp.where(sub == rows - 1, halo, roll(adj[3, z], -1, 0)))
        halo = jnp.broadcast_to(gu[z : z + 1, :], (rows, cols))
        p.append(jnp.where(sub == 0, halo, roll(adj[4, z], 1, 0)))
        p.append(adj[5, z + 1] if z + 1 < layers else above)
        p.append(adj[6, z - 1] if z > 0 else below)
        mean = WEIGHT7[0] * p[0] + WEIGHT7[1] * (p[1] + p[2] + p[3] + p[4] + p[5] + p[6])
        dot = (
            wide[z] * (p[1] - p[2])
            + wide[layers + z] * (p[3] - p[4])
            + wide[2 * layers + z] * (p[5] - p[6])
        )
        common = omega * (mean + 4.0 * WEIGHT7[1] * dot)
        if z == 0:
            common = common + heated
        for j in range(7):
            out[j, z] = (1.0 - omega) * p[j] + common


def per_device(populations, cell_type, adjoint, sizes):
    nx, ny, nz = sizes
    axes = ("gx", "gy", "gz")

    def along(delta_x, delta_y):
        moves = []
        for a in range(nx):
            for b in range(ny * nz):
                a2, b2 = a + delta_x, b + delta_y
                if 0 <= a2 < nx and 0 <= b2 < ny * nz:
                    moves.append((a * ny * nz + b, a2 * ny * nz + b2))
        return moves

    def across(delta):
        moves = []
        for a in range(nx):
            for b in range(ny):
                for c in range(nz):
                    if 0 <= b + delta < ny:
                        moves.append(((a * ny + b) * nz + c, (a * ny + b + delta) * nz + c))
        return moves

    _, rows, cols = cell_type.shape
    layers, heat_rows = adjoint.shape[1:3]
    post, ysh, xp, xm, yp, ym, gp, gm = pl.pallas_call(
        collide_kernel,
        out_shape=(
            f32(19, TOP, rows, cols),
            f32(10, TOP, rows, cols),
            f32(heat_rows, LANES),
            f32(heat_rows, LANES),
            f32(Y_ROWS, cols),
            f32(Y_ROWS, cols),
            f32(layers, cols),
            f32(layers, cols),
        ),
        in_specs=[pl.BlockSpec(memory_space=pltpu.HBM)] * 3,
        out_specs=(VMEM,) * 8,
        scratch_shapes=[
            pltpu.VMEM((19, TOP, rows, cols), jnp.float32),
            pltpu.VMEM((1, rows, cols), jnp.int32),
            pltpu.VMEM(adjoint.shape, jnp.float32),
            pltpu.SemaphoreType.DMA((4,)),
        ],
        compiler_params=pltpu.CompilerParams(vmem_limit_bytes=16 << 20),
        name="collide",
    )(*(pltpu.with_memory_space_constraint(a, pltpu.HBM) for a in (populations, cell_type, adjoint)))
    xl = lax.ppermute(xp, axes, along(1, 0))
    xr = lax.ppermute(xm, axes, along(-1, 0))
    gu = lax.ppermute(gp, axes, across(1))
    gd = lax.ppermute(gm, axes, across(-1))
    top = jnp.concatenate([xl[rows - 1 : rows], xr[rows - 1 : rows]], axis=1)
    bottom = jnp.concatenate([xl[0:1], xr[0:1]], axis=1)
    yp = lax.dynamic_update_slice(yp, top, (CORNER_ROW, 0))
    ym = lax.dynamic_update_slice(ym, bottom, (CORNER_ROW, 0))
    yu = lax.ppermute(yp, axes, along(0, 1))
    yd = lax.ppermute(ym, axes, along(0, -1))
    flow_next, vel = pl.pallas_call(
        stream_kernel,
        out_shape=(f32(*populations.shape), f32(nz, 3 * layers + 1, rows, cols)),
        in_specs=[VMEM] * 8,
        out_specs=(VMEM,) * 2,
        scratch_shapes=[pltpu.VMEM((2, 8, LANES), jnp.float32)],
        compiler_params=pltpu.CompilerParams(vmem_limit_bytes=16 << 20),
        name="stream",
    )(post, ysh, populations, cell_type, xl, xr, yu, yd)
    va = lax.all_to_all(vel, "gz", split_axis=0, concat_axis=0, tiled=True)
    adjoint_prev = pl.pallas_call(
        functools.partial(thermal_kernel, nz),
        out_shape=f32(*adjoint.shape),
        in_specs=[VMEM] * 8,
        out_specs=VMEM,
        scratch_shapes=[pltpu.VMEM((3 * layers + 1, heat_rows, cols), jnp.float32)],
        compiler_params=pltpu.CompilerParams(vmem_limit_bytes=16 << 20),
        name="thermal",
    )(adjoint, va, xl, xr, yu, yd, gu, gd)
    return flow_next, adjoint_prev


def solution(mesh):
    sizes = tuple(mesh.shape[axis] for axis in ("gx", "gy", "gz"))
    placed = (
        P(None, None, ("gy", "gz"), "gx"),
        P(None, ("gy", "gz"), "gx"),
        P(None, "gz", "gy", "gx"),
    )

    def body(p, c, a):
        return per_device(p, c, a, sizes)

    return jax.shard_map(
        body,
        mesh=mesh,
        in_specs=placed,
        out_specs=(P(None, None, ("gy", "gz"), "gx"), P(None, "gz", "gy", "gx")),
        check_vma=False,
    )
```

```python
import jax
import jax.numpy as jnp
from jax import lax
from jax.experimental import pallas as pl
from jax.experimental.pallas import tpu as pltpu
from jax.sharding import PartitionSpec as P


VEL19 = [
    (0, 0, 0),
    (1, 0, 0),
    (-1, 0, 0),
    (0, 1, 0),
    (0, -1, 0),
    (0, 0, 1),
    (0, 0, -1),
    (1, 1, 0),
    (-1, -1, 0),
    (1, -1, 0),
    (-1, 1, 0),
    (1, 0, 1),
    (-1, 0, -1),
    (1, 0, -1),
    (-1, 0, 1),
    (0, 1, 1),
    (0, -1, -1),
    (0, 1, -1),
    (0, -1, 1),
]
WEIGHT19 = [1.0 / 3.0] + [1.0 / 18.0] * 6 + [1.0 / 36.0] * 12
OPPOSITE = [0, 2, 1, 4, 3, 6, 5, 8, 7, 10, 9, 12, 11, 14, 13, 16, 15, 18, 17]
WEIGHT7 = [0.25] + [0.125] * 6
OMEGA_FLOW = 1.6
OMEGA_FLUID = 1.25
OMEGA_SOLID = 1.6

BASE = 8
TOP = 8
LANES = 128
XP = [1, 7, 9, 11, 13]
XM = [2, 8, 10, 12, 14]
YP = [3, 7, 10, 15, 17]
YM = [4, 8, 9, 16, 18]
YALL = YP + YM
FLAG_LANE = 40
HEAT_LANE = 64
FLAG_ROW = 40
CORNER_ROW = 41
CODE_ROW = 42
HEAT_ROW = 48
Y_ROWS = 64
VMEM = pl.BlockSpec(memory_space=pltpu.VMEM)


def f32(*shape):
    return jax.ShapeDtypeStruct(shape, jnp.float32)


def iota(shape, axis):
    return lax.broadcasted_iota(jnp.int32, shape, axis)


def roll(value, shift, axis=1):
    size = value.shape[axis]
    shift = shift % size
    return value if shift == 0 else pltpu.roll(value, shift, axis)


def collide_kernel(
    pops_in, cells_in, adj_in, post, ysh, xa, xb, ya, yb, ga, gb, pops, cells, adj, faces, sem
):
    rows, cols = cells.shape[1:]
    odd_x, odd_g, odd_y = (lax.axis_index(axis) % 2 for axis in ("gx", "gy", "gz"))
    yp, ym = faces.at[0], faces.at[1]
    half = TOP // 2
    loads = [
        pltpu.make_async_copy(cells_in.at[BASE], cells.at[0], sem.at[0]),
        pltpu.make_async_copy(
            pops_in.at[:, BASE : BASE + half], pops.at[:, 0:half], sem.at[1]
        ),
        pltpu.make_async_copy(
            pops_in.at[:, BASE + half : BASE + TOP], pops.at[:, half:TOP], sem.at[2]
        ),
        pltpu.make_async_copy(adj_in, adj, sem.at[3]),
        pltpu.make_async_copy(cells_in.at[0], cells.at[1], sem.at[4]),
    ]
    for load in loads:
        load.start()
    loads[0].wait()
    left, right = slice(0, LANES), slice(cols - LANES, cols)
    lane = iota((rows, LANES), 1)
    fluid = jnp.where(cells[0] == 0, 1.0, 0.0)
    to_right = jnp.where(lane == FLAG_LANE, roll(fluid[:, right], FLAG_LANE + 1), 0.0)
    to_left = jnp.where(lane == FLAG_LANE, roll(fluid[:, left], FLAG_LANE), 0.0)
    yp[FLAG_ROW : FLAG_ROW + 1, :] = fluid[rows - 1 : rows]
    ym[FLAG_ROW : FLAG_ROW + 1, :] = fluid[0:1]
    for level in range(TOP):
        if level % half == 0:
            loads[1 + level // half].wait()
        f = [pops[i, level] for i in range(19)]
        density = sum(f[1:], f[0])
        u = []
        for k in range(3):
            plus = sum(f[i] for i in range(19) if VEL19[i][k] == 1)
            minus = sum(f[i] for i in range(19) if VEL19[i][k] == -1)
            u.append((plus - minus) / density)
        common = 1.0 - 1.5 * (u[0] * u[0] + u[1] * u[1] + u[2] * u[2])
        scaled = OMEGA_FLOW * density
        for i in range(19):
            c = VEL19[i]
            cu = None
            for k in range(3):
                if c[k]:
                    term = u[k] if c[k] == 1 else -u[k]
                    cu = term if cu is None else cu + term
            shape = common if cu is None else common + cu * (3.0 + 4.5 * cu)
            out = (1.0 - OMEGA_FLOW) * f[i] + (WEIGHT19[i] * scaled) * shape
            post[i, level] = out
            if i in XP:
                at = XP.index(i) * TOP + level
                to_right = jnp.where(lane == at, roll(out[:, right], at + 1), to_right)
            if i in XM:
                at = XM.index(i) * TOP + level
                to_left = jnp.where(lane == at, roll(out[:, left], at), to_left)
            if i in YP:
                at = YP.index(i) * TOP + level
                yp[at : at + 1, :] = out[rows - 1 : rows]
                ysh[YALL.index(i), level, 1:rows, :] = out[0 : rows - 1]
            if i in YM:
                at = YM.index(i) * TOP + level
                ym[at : at + 1, :] = out[0:1]
                ysh[YALL.index(i), level, 0 : rows - 1, :] = out[1:rows]
    loads[3].wait()
    layers, arows = adj.shape[1:3]
    lane = iota((arows, LANES), 1)
    heat_right = jnp.zeros((arows, LANES), jnp.float32)
    heat_left = heat_right
    for z in range(layers):
        at = HEAT_LANE + z
        heat_right = jnp.where(lane == at, roll(adj[2, z, :, right], at + 1), heat_right)
        heat_left = jnp.where(lane == at, roll(adj[1, z, :, left], at), heat_left)
        high, low = adj[4, z, arows - 1 : arows, :], adj[3, z, 0:1, :]
        ga[z : z + 1, :] = jnp.where(odd_g == 0, high, low)
        gb[z : z + 1, :] = jnp.where(odd_g == 0, low, high)
    xa[...] = jnp.where(odd_x == 0, heat_right, heat_left)
    xb[...] = jnp.where(odd_x == 0, heat_left, heat_right)
    lane = iota((rows, LANES), 1)
    to_right = jnp.where(lane < HEAT_LANE, to_right, heat_right[0:rows])
    to_left = jnp.where(lane < HEAT_LANE, to_left, heat_left[0:rows])
    xa[0:rows, :] = jnp.where(odd_x == 0, to_right, to_left)
    xb[0:rows, :] = jnp.where(odd_x == 0, to_left, to_right)
    yp[HEAT_ROW : HEAT_ROW + arows, :] = adj[6, layers - 1]
    ym[HEAT_ROW : HEAT_ROW + arows, :] = adj[5, 0]
    loads[4].wait()
    code = jnp.where(cells[1] == 2, 1.0, 0.0)
    yp[CODE_ROW : CODE_ROW + rows, :] = code
    ym[CODE_ROW : CODE_ROW + rows, :] = code
    ya[...] = faces[odd_y]
    yb[...] = faces[1 - odd_y]


def stream_kernel(
    post, ysh, pops, cells, xa, xb, ya, yb, out, pa, pb, pc, own, ext, halos, vel
):
    rows, cols = cells.shape[1:]
    odd_x, odd_y = (lax.axis_index(axis) % 2 for axis in ("gx", "gz"))
    gz = lax.axis_index("gz")
    xl = jnp.where(odd_x == 0, xb[...], xa[...])
    xr = jnp.where(odd_x == 0, xa[...], xb[...])
    first, second = ya[0:HEAT_ROW, :], yb[0:HEAT_ROW, :]
    halos[0] = jnp.where(odd_y == 0, second, first)
    halos[1] = jnp.where(odd_y == 0, first, second)
    yu, yd = halos.at[0], halos.at[1]
    last = cols - LANES
    sub = iota((rows, cols), 0)
    col = iota((rows, LANES), 1)

    ext[0, 0:1, :] = yu[CORNER_ROW : CORNER_ROW + 1, 0:LANES]
    ext[1, 0:1, :] = yu[CORNER_ROW : CORNER_ROW + 1, LANES : 2 * LANES]
    ext[0, 1 : rows + 1, :] = xl[0:rows, :]
    ext[1, 1 : rows + 1, :] = xr[0:rows, :]
    ext[0, rows + 1 : rows + 2, :] = yd[CORNER_ROW : CORNER_ROW + 1, 0:LANES]
    ext[1, rows + 1 : rows + 2, :] = yd[CORNER_ROW : CORNER_ROW + 1, LANES : 2 * LANES]
    beyond = {
        (side, cy): ext[side, 1 - cy : 1 - cy + rows, :] for side in (0, 1) for cy in (-1, 0, 1)
    }

    def shift_x(value, cx, cy, lane_at):
        if cx == 0:
            return value
        value = roll(value, cx)
        if cx == 1:
            edge = roll(beyond[0, cy], -lane_at)
            patched = jnp.where(col == 0, edge, value[:, 0:LANES])
            return jnp.concatenate([patched, value[:, LANES:]], axis=1)
        edge = roll(beyond[1, cy], LANES - 1 - lane_at)
        patched = jnp.where(col == LANES - 1, edge, value[:, last:])
        return jnp.concatenate([value[:, 0:last], patched], axis=1)

    def shift_y(value, cy, halo):
        if cy == 0:
            return value
        halo = jnp.broadcast_to(halo, (rows, cols))
        return jnp.where(sub == (0 if cy == 1 else rows - 1), halo, value)

    fluid = jnp.where(cells[BASE] == 0, 1.0, 0.0)
    is_fluid = fluid > 0.5
    spread = {0: fluid}
    spread[1] = shift_y(
        jnp.concatenate([fluid[rows - 1 : rows], fluid[0 : rows - 1]], axis=0),
        1,
        yu[FLAG_ROW : FLAG_ROW + 1, :],
    )
    spread[-1] = shift_y(
        jnp.concatenate([fluid[1:rows], fluid[0:1]], axis=0), -1, yd[FLAG_ROW : FLAG_ROW + 1, :]
    )
    open_from = {
        (cx, cy): shift_x(spread[cy], cx, cy, FLAG_LANE) > 0.5
        for cx in (-1, 0, 1)
        for cy in (-1, 0, 1)
    }

    out[:, 0:BASE] = pops[:, 0:BASE]
    layers = own.shape[0] // 3
    for level in range(TOP):
        density = None
        momentum = [None, None, None]
        for i in range(19):
            cx, cy, cz = VEL19[i]
            before = pops[i, BASE + level]
            back = post[OPPOSITE[i], level]
            source = level - cz
            if i == 0:
                pulled = back
            elif source < 0 or source >= TOP:
                pulled = back
            else:
                if cy == 0:
                    value = post[i, source]
                else:
                    at = (YP if cy == 1 else YM).index(i) * TOP + source
                    halo = (yu if cy == 1 else yd)[at : at + 1, :]
                    value = shift_y(ysh[YALL.index(i), source], cy, halo)
                if cx:
                    value = shift_x(value, cx, cy, (XP if cx == 1 else XM).index(i) * TOP + source)
                pulled = jnp.where(open_from[cx, cy], value, back)
            new = jnp.where(is_fluid, pulled, before)
            out[i, BASE + level] = new
            density = new if density is None else density + new
            for k in range(3):
                c = VEL19[i][k]
                if c:
                    term = new if c == 1 else -new
                    momentum[k] = term if momentum[k] is None else momentum[k] + term
        for k in range(3):
            vel[level // layers, k * layers + level % layers] = jnp.where(
                is_fluid, momentum[k] / density, 0.0
            )
    code = jnp.where(cells[0] == 2, 1.0, 0.0)
    passed = yd[CODE_ROW : CODE_ROW + rows, :]
    for buffer, lower in ((pa, 1), (pb, 0), (pc, 3), (own, 2)):
        buffer[0 : 3 * layers] = vel[jnp.where(gz == lower, 0, 1)]
    pa[3 * layers] = jnp.where(gz == 3, code, fluid)
    pb[3 * layers] = fluid
    pc[3 * layers] = jnp.where(gz == 1, passed, fluid)
    own[3 * layers] = jnp.where(gz == 0, code, fluid)


def thermal_kernel(adj, pa, pb, pc, own, xa, xb, ya, yb, ga, gb, out, wide):
    layers, rows, cols = adj.shape[1:]
    odd_x, odd_g, odd_y = (lax.axis_index(axis) % 2 for axis in ("gx", "gy", "gz"))
    gz = lax.axis_index("gz")
    planes, part = own.shape[:2]
    last = cols - LANES
    at_two, at_zero = gz == 2, gz == 0
    for q in range(planes):
        a, b, c, mine = pa[q], pb[q], pc[q], own[q]
        blocks = [
            jnp.where(at_two, b, a),
            jnp.where(at_two, a, b),
            jnp.where(at_two, mine, c),
            jnp.where(at_two, c, mine),
        ]
        if q == planes - 1:
            near = ya[CODE_ROW : CODE_ROW + part, :]
            blocks = [jnp.where(at_zero, v, w) for v, w in zip((mine, near, c, a), blocks)]
        for s in range(4):
            wide[q, part * s : part * (s + 1), :] = blocks[s]
    sub = iota((rows, cols), 0)
    col = iota((rows, LANES), 1)
    mark = wide[planes - 1]
    is_fluid = (mark * jnp.where(gz >= 2, 1.0, 0.0)) > 0.5
    heated = mark * jnp.where(at_zero, 1.0, 0.0)
    xl = jnp.where(odd_x == 0, xb[...], xa[...])
    xr = jnp.where(odd_x == 0, xa[...], xb[...])
    gu = jnp.where(odd_g == 0, gb[...], ga[...])
    gd = jnp.where(odd_g == 0, ga[...], gb[...])
    first, second = ya[HEAT_ROW : HEAT_ROW + rows, :], yb[HEAT_ROW : HEAT_ROW + rows, :]
    below = jnp.where(at_zero, 0.0, jnp.where(odd_y == 0, second, first))
    above = jnp.where(gz == 3, 0.0, jnp.where(odd_y == 0, first, second))
    omega = jnp.where(is_fluid, OMEGA_FLUID, OMEGA_SOLID)
    for z in range(layers):
        p = [adj[0, z]]
        ahead = roll(adj[1, z], -1)
        edge = roll(xr, LANES - 1 - (HEAT_LANE + z))
        p.append(
            jnp.concatenate(
                [ahead[:, 0:last], jnp.where(col == LANES - 1, edge, ahead[:, last:])], axis=1
            )
        )
        behind = roll(adj[2, z], 1)
        edge = roll(xl, -(HEAT_LANE + z))
        p.append(
            jnp.concatenate(
                [jnp.where(col == 0, edge, behind[:, 0:LANES]), behind[:, LANES:]], axis=1
            )
        )
        halo = jnp.broadcast_to(gd[z : z + 1, :], (rows, cols))
        p.append(jnp.where(sub == rows - 1, halo, roll(adj[3, z], -1, 0)))
        halo = jnp.broadcast_to(gu[z : z + 1, :], (rows, cols))
        p.append(jnp.where(sub == 0, halo, roll(adj[4, z], 1, 0)))
        p.append(adj[5, z + 1] if z + 1 < layers else above)
        p.append(adj[6, z - 1] if z > 0 else below)
        mean = WEIGHT7[0] * p[0] + WEIGHT7[1] * (p[1] + p[2] + p[3] + p[4] + p[5] + p[6])
        dot = (
            wide[z] * (p[1] - p[2])
            + wide[layers + z] * (p[3] - p[4])
            + wide[2 * layers + z] * (p[5] - p[6])
        )
        common = omega * (mean + 4.0 * WEIGHT7[1] * jnp.where(is_fluid, dot, 0.0))
        if z == 0:
            common = common + heated
        for j in range(7):
            out[j, z] = (1.0 - omega) * p[j] + common


def per_device(populations, cell_type, adjoint, sizes):
    nx, ny, nz = sizes
    axes = ("gx", "gy", "gz")

    def swaps(axis, size, parity):
        moves = []
        for a in range(nx):
            for b in range(ny):
                for c in range(nz):
                    place = (a, b, c, b * nz + c)[axis]
                    other = place + 1 if (place - parity) % 2 == 0 else place - 1
                    if 0 <= other < size:
                        there = {0: (other, b, c), 1: (a, other, c), 3: (a, other // nz, other % nz)}[axis]
                        moves.append(
                            ((a * ny + b) * nz + c, (there[0] * ny + there[1]) * nz + there[2])
                        )
        return moves

    def inside(pairs):
        return [(g * nz + i, g * nz + j) for g in range(nx * ny) for i, j in pairs]

    _, rows, cols = cell_type.shape
    layers, heat_rows = adjoint.shape[1:3]
    post, ysh, xa, xb, ya, yb, ga, gb = pl.pallas_call(
        collide_kernel,
        out_shape=(
            f32(19, TOP, rows, cols),
            f32(10, TOP, rows, cols),
            f32(heat_rows, LANES),
            f32(heat_rows, LANES),
            f32(Y_ROWS, cols),
            f32(Y_ROWS, cols),
            f32(layers, cols),
            f32(layers, cols),
        ),
        in_specs=[pl.BlockSpec(memory_space=pltpu.HBM)] * 3,
        out_specs=(VMEM,) * 8,
        scratch_shapes=[
            pltpu.VMEM((19, TOP, rows, cols), jnp.float32),
            pltpu.VMEM((2, rows, cols), jnp.int32),
            pltpu.VMEM(adjoint.shape, jnp.float32),
            pltpu.VMEM((2, Y_ROWS, cols), jnp.float32),
            pltpu.SemaphoreType.DMA((5,)),
        ],
        compiler_params=pltpu.CompilerParams(vmem_limit_bytes=16 << 20),
        name="collide",
    )(*(pltpu.with_memory_space_constraint(a, pltpu.HBM) for a in (populations, cell_type, adjoint)))

    def move(value, pairs):
        return lax.ppermute(value, axes, pairs)

    xa = move(xa, swaps(0, nx, 0))
    xb = move(xb, swaps(0, nx, 1))
    ga = move(ga, swaps(1, ny, 0))
    gb = move(gb, swaps(1, ny, 1))
    odd_x, odd_y = (lax.axis_index(axis) % 2 for axis in ("gx", "gz"))

    def corners(row):
        first, second = xa[row : row + 1], xb[row : row + 1]
        return jnp.where(
            odd_x == 0,
            jnp.concatenate([second, first], axis=1),
            jnp.concatenate([first, second], axis=1),
        )

    high, low = corners(rows - 1), corners(0)
    ya = lax.dynamic_update_slice(ya, jnp.where(odd_y == 0, high, low), (CORNER_ROW, 0))
    yb = lax.dynamic_update_slice(yb, jnp.where(odd_y == 0, low, high), (CORNER_ROW, 0))
    ya = move(ya, swaps(3, ny * nz, 0))
    yb = move(yb, swaps(3, ny * nz, 1))
    planes = f32(3 * layers + 1, rows, cols)
    flow_next, pa, pb, pc, own = pl.pallas_call(
        stream_kernel,
        out_shape=(f32(*populations.shape), planes, planes, planes, planes),
        in_specs=[VMEM] * 8,
        out_specs=(VMEM,) * 5,
        scratch_shapes=[
            pltpu.VMEM((2, 8, LANES), jnp.float32),
            pltpu.VMEM((2, HEAT_ROW, cols), jnp.float32),
            pltpu.VMEM((2, 3 * layers, rows, cols), jnp.float32),
        ],
        compiler_params=pltpu.CompilerParams(vmem_limit_bytes=16 << 20),
        name="stream",
    )(post, ysh, populations, cell_type, xa, xb, ya, yb)
    pa = move(pa, inside(((1, 2), (0, 3), (3, 0))))
    pb = move(pb, inside(((0, 2), (1, 3))))
    pc = move(pc, inside(((2, 3), (3, 2), (1, 0))))
    adjoint_prev = pl.pallas_call(
        thermal_kernel,
        out_shape=f32(*adjoint.shape),
        in_specs=[VMEM] * 11,
        out_specs=VMEM,
        scratch_shapes=[pltpu.VMEM((3 * layers + 1, heat_rows, cols), jnp.float32)],
        compiler_params=pltpu.CompilerParams(vmem_limit_bytes=16 << 20),
        name="thermal",
    )(adjoint, pa, pb, pc, own, xa, xb, ya, yb, ga, gb)
    return flow_next, adjoint_prev


def solution(mesh):
    sizes = tuple(mesh.shape[axis] for axis in ("gx", "gy", "gz"))
    placed = (
        P(None, None, ("gy", "gz"), "gx"),
        P(None, ("gy", "gz"), "gx"),
        P(None, "gz", "gy", "gx"),
    )

    def body(p, c, a):
        return per_device(p, c, a, sizes)

    return jax.shard_map(
        body,
        mesh=mesh,
        in_specs=placed,
        out_specs=(P(None, None, ("gy", "gz"), "gx"), P(None, "gz", "gy", "gx")),
        check_vma=False,
    )
```

```python
import functools

import jax
import jax.numpy as jnp
from jax import lax
from jax.experimental import pallas as pl
from jax.experimental.pallas import tpu as pltpu
from jax.sharding import PartitionSpec as P


VEL19 = [
    (0, 0, 0),
    (1, 0, 0),
    (-1, 0, 0),
    (0, 1, 0),
    (0, -1, 0),
    (0, 0, 1),
    (0, 0, -1),
    (1, 1, 0),
    (-1, -1, 0),
    (1, -1, 0),
    (-1, 1, 0),
    (1, 0, 1),
    (-1, 0, -1),
    (1, 0, -1),
    (-1, 0, 1),
    (0, 1, 1),
    (0, -1, -1),
    (0, 1, -1),
    (0, -1, 1),
]
WEIGHT19 = [1.0 / 3.0] + [1.0 / 18.0] * 6 + [1.0 / 36.0] * 12
OPPOSITE = [0, 2, 1, 4, 3, 6, 5, 8, 7, 10, 9, 12, 11, 14, 13, 16, 15, 18, 17]
WEIGHT7 = [0.25] + [0.125] * 6
OMEGA_FLOW = 1.6
OMEGA_FLUID = 1.25
OMEGA_SOLID = 1.6

BASE = 8
TOP = 8
LANES = 128
XP = [1, 7, 9, 11, 13]
XM = [2, 8, 10, 12, 14]
YP = [3, 7, 10, 15, 17]
YM = [4, 8, 9, 18, 16]
YALL = YP + YM
FLAG_LANE = 40
HEAT_LANE = 64
FLAG_ROW = 31
CORNER_ROW = 32
HEAT_ROW = 40
Y_ROWS = 56
VMEM = pl.BlockSpec(memory_space=pltpu.VMEM)


def f32(*shape):
    return jax.ShapeDtypeStruct(shape, jnp.float32)


def iota(shape, axis):
    return lax.broadcasted_iota(jnp.int32, shape, axis)


def roll(value, shift, axis=1):
    size = value.shape[axis]
    shift = shift % size
    return value if shift == 0 else pltpu.roll(value, shift, axis)


def collide_kernel(
    pops_in, cells_in, adj_in, post, ysh, xp, xm, yp, ym, gp, gm, faces, pops, cells, adj, sem
):
    rows, cols = cells.shape[1:]
    half = TOP // 2
    loads = [
        pltpu.make_async_copy(cells_in.at[BASE], cells.at[0], sem.at[0]),
        pltpu.make_async_copy(
            pops_in.at[:, BASE : BASE + half], pops.at[:, 0:half], sem.at[1]
        ),
        pltpu.make_async_copy(
            pops_in.at[:, BASE + half : BASE + TOP], pops.at[:, half:TOP], sem.at[2]
        ),
        pltpu.make_async_copy(adj_in, adj, sem.at[3]),
    ]
    for load in loads:
        load.start()
    loads[0].wait()
    left, right = slice(0, LANES), slice(cols - LANES, cols)
    lane = iota((rows, LANES), 1)
    fluid = jnp.where(cells[0] == 0, 1.0, 0.0)
    to_right = jnp.where(lane == FLAG_LANE, roll(fluid[:, right], FLAG_LANE + 1), 0.0)
    to_left = jnp.where(lane == FLAG_LANE, roll(fluid[:, left], FLAG_LANE), 0.0)
    for level in range(TOP):
        if level % half == 0:
            loads[1 + level // half].wait()
        f = [pops[i, level] for i in range(19)]
        density = sum(f[1:], f[0])
        u = []
        for k in range(3):
            plus = sum(f[i] for i in range(19) if VEL19[i][k] == 1)
            minus = sum(f[i] for i in range(19) if VEL19[i][k] == -1)
            u.append((plus - minus) / density)
        common = 1.0 - 1.5 * (u[0] * u[0] + u[1] * u[1] + u[2] * u[2])
        scaled = OMEGA_FLOW * density
        for i in range(19):
            c = VEL19[i]
            cu = None
            for k in range(3):
                if c[k]:
                    term = u[k] if c[k] == 1 else -u[k]
                    cu = term if cu is None else cu + term
            shape = common if cu is None else common + cu * (3.0 + 4.5 * cu)
            out = (1.0 - OMEGA_FLOW) * f[i] + (WEIGHT19[i] * scaled) * shape
            post[i, level] = out
            if i in XP:
                at = XP.index(i) * TOP + level
                to_right = jnp.where(lane == at, roll(out[:, right], at + 1), to_right)
            if i in XM:
                at = XM.index(i) * TOP + level
                to_left = jnp.where(lane == at, roll(out[:, left], at), to_left)
            if i in YP:
                at = YP.index(i) * TOP + level
                faces[0, at : at + 1, :] = out[rows - 1 : rows]
                ysh[YALL.index(i), level, 1:rows, :] = out[0 : rows - 1]
            if i in YM:
                at = YM.index(i) * TOP + level
                faces[1, at : at + 1, :] = out[0:1]
                ysh[YALL.index(i), level, 0 : rows - 1, :] = out[1:rows]
    loads[3].wait()
    layers, arows = adj.shape[1:3]
    packed = arows // 2
    heat_right = jnp.zeros((packed, LANES), jnp.float32)
    heat_left = heat_right
    lane = iota((packed, LANES), 1)
    for z in range(layers):
        for part in range(2):
            at = HEAT_LANE + part * layers + z
            block = slice(part * packed, (part + 1) * packed)
            heat_right = jnp.where(lane == at, roll(adj[2, z, block, right], at + 1), heat_right)
            heat_left = jnp.where(lane == at, roll(adj[1, z, block, left], at), heat_left)
        gp[z : z + 1, :] = adj[4, z, arows - 1 : arows, :]
        gm[z : z + 1, :] = adj[3, z, 0:1, :]
    xp[...] = heat_right
    xm[...] = heat_left
    lane = iota((rows, LANES), 1)
    xp[0:rows, :] = jnp.where(lane < HEAT_LANE, to_right, heat_right[0:rows])
    xm[0:rows, :] = jnp.where(lane < HEAT_LANE, to_left, heat_left[0:rows])
    yp[0:HEAT_ROW, :] = faces[0]
    ym[0:HEAT_ROW, :] = faces[1]
    yp[FLAG_ROW : FLAG_ROW + 1, :] = fluid[rows - 1 : rows]
    ym[FLAG_ROW : FLAG_ROW + 1, :] = fluid[0:1]
    yp[HEAT_ROW : HEAT_ROW + arows, :] = adj[6, layers - 1]
    ym[HEAT_ROW : HEAT_ROW + arows, :] = adj[5, 0]


def own_fluid(cells):
    return jnp.where(cells[BASE] == 0, 1.0, 0.0)


def shifted(value, cx, left, right):
    if cx == 0:
        return value
    col = iota((value.shape[0], LANES), 1)
    value = roll(value, cx)
    if cx == 1:
        patched = jnp.where(col == 0, left, value[:, 0:LANES])
        return jnp.concatenate([patched, value[:, LANES:]], axis=1)
    last = value.shape[1] - LANES
    patched = jnp.where(col == LANES - 1, right, value[:, last:])
    return jnp.concatenate([value[:, 0:last], patched], axis=1)


def columns_beyond(ext, xl, xr, rows, yu=None, yd=None):
    zero = jnp.zeros((1, LANES), jnp.float32)
    for side, own in ((0, xl), (1, xr)):
        part = slice(side * LANES, (side + 1) * LANES)
        ext[side, 0:1, :] = zero if yu is None else yu[CORNER_ROW : CORNER_ROW + 1, part]
        ext[side, 1 : rows + 1, :] = own[0:rows, :]
        ext[side, rows + 1 : rows + 2, :] = zero if yd is None else yd[CORNER_ROW : CORNER_ROW + 1, part]
    return {
        (side, cy): ext[side, 1 - cy : 1 - cy + rows, :] for side in (0, 1) for cy in (-1, 0, 1)
    }


def pull(post, ysh, cells, xl, xr, ext, visit, yu=None, yd=None):
    rows, cols = cells.shape[1:]
    sub = iota((rows, cols), 0)
    beyond = columns_beyond(ext, xl, xr, rows, yu, yd)

    def shift_x(value, cx, cy, lane_at):
        if cx == 1:
            return shifted(value, 1, roll(beyond[0, cy], -lane_at), None)
        if cx == -1:
            return shifted(value, -1, None, roll(beyond[1, cy], LANES - 1 - lane_at))
        return value

    def halo_row(value, cy, at):
        if cy == 0 or yu is None:
            return value
        halo = jnp.broadcast_to((yu if cy == 1 else yd)[at : at + 1, :], (rows, cols))
        return jnp.where(sub == (0 if cy == 1 else rows - 1), halo, value)

    fluid = own_fluid(cells)
    spread = {
        0: fluid,
        1: halo_row(jnp.concatenate([fluid[rows - 1 : rows], fluid[0 : rows - 1]], axis=0), 1, FLAG_ROW),
        -1: halo_row(jnp.concatenate([fluid[1:rows], fluid[0:1]], axis=0), -1, FLAG_ROW),
    }
    open_from = {
        (cx, cy): shift_x(spread[cy], cx, cy, FLAG_LANE) > 0.5
        for cx in (-1, 0, 1)
        for cy in (-1, 0, 1)
    }
    for level in range(TOP):
        for i in range(19):
            cx, cy, cz = VEL19[i]
            back = post[OPPOSITE[i], level]
            source = level - cz
            if i == 0 or source < 0 or source >= TOP:
                visit(level, i, back)
                continue
            if cy == 0:
                value = post[i, source]
            else:
                at = (YP if cy == 1 else YM).index(i) * TOP + source
                value = halo_row(ysh[YALL.index(i), source], cy, at)
            if cx:
                value = shift_x(value, cx, cy, (XP if cx == 1 else XM).index(i) * TOP + source)
            visit(level, i, jnp.where(open_from[cx, cy], value, back))


def add_to(sums, i, value):
    density, momentum = sums
    density = value if density is None else density + value
    momentum = list(momentum)
    for k in range(3):
        c = VEL19[i][k]
        if c:
            term = value if c == 1 else -value
            momentum[k] = term if momentum[k] is None else momentum[k] + term
    return density, momentum


def inner_velocity_kernel(post, ysh, cells, xl, xr, vel, edge, ext):
    rows, cols = cells.shape[1:]
    sub = iota((rows, cols), 0)
    is_fluid = own_fluid(cells) > 0.5
    vel[0] = jnp.zeros(vel.shape[1:], jnp.float32)
    vel[1] = jnp.zeros(vel.shape[1:], jnp.float32)
    layers = (vel.shape[1] - 1) // 3
    vel[0, 3 * layers] = jnp.where(cells[0] == 2, 1.0, 0.0)
    vel[2, 3 * layers] = own_fluid(cells)
    vel[3, 3 * layers] = own_fluid(cells)
    state = {}

    def visit(level, i, pulled):
        cy = VEL19[i][1]
        if cy:
            pulled = jnp.where(sub == (0 if cy == 1 else rows - 1), 0.0, pulled)
        sums = add_to(state.get(level, (None, [None] * 3)), i, pulled)
        state[level] = sums
        if i == 18:
            density, momentum = sums
            for k, part in enumerate([density] + momentum):
                edge[0, k, level : level + 1, :] = part[0:1]
                edge[1, k, level : level + 1, :] = part[rows - 1 : rows]
            for k in range(3):
                vel[2 + level // layers, k * layers + level % layers] = jnp.where(
                    is_fluid, momentum[k] / density, 0.0
                )

    pull(post, ysh, cells, xl, xr, ext, visit)


def edge_velocity_kernel(vel_in, edge, cells, faces, yu, yd, vel):
    rows, cols = cells.shape[1:]
    layers = (vel.shape[1] - 1) // 3
    sub, lane = iota((TOP, cols), 0), iota((TOP, LANES), 1)
    fluid = own_fluid(cells)
    vel[...] = vel_in[...]
    for side, (row, cy, pops, source, mine) in enumerate(
        ((0, 1, YP, yu, 1), (rows - 1, -1, YM, yd, 0))
    ):
        is_fluid = jnp.broadcast_to(fluid[row : row + 1], (TOP, cols)) > 0.5
        corner = [
            jnp.broadcast_to(source[CORNER_ROW : CORNER_ROW + 1, part], (TOP, LANES))
            for part in (slice(0, LANES), slice(LANES, 2 * LANES))
        ]
        flags = jnp.broadcast_to(source[FLAG_ROW : FLAG_ROW + 1, :], (TOP, cols))
        open_from = {
            0: flags > 0.5,
            1: shifted(flags, 1, roll(corner[0], -FLAG_LANE), None) > 0.5,
            -1: shifted(flags, -1, None, roll(corner[1], LANES - 1 - FLAG_LANE)) > 0.5,
        }
        sums = (edge[side, 0], [edge[side, 1], edge[side, 2], edge[side, 3]])
        for at, i in enumerate(pops):
            cx, _, cz = VEL19[i]
            value = source[at * TOP : (at + 1) * TOP, :]
            if cx:
                first = (XP if cx == 1 else XM).index(i) * TOP
                column = corner[0 if cx == 1 else 1]
                entry = jnp.zeros((TOP, LANES), jnp.float32)
                goal = 0 if cx == 1 else LANES - 1
                level_of = iota((TOP, LANES), 0)
                for level in range(TOP):
                    entry = jnp.where(level_of == level, roll(column, goal - first - level), entry)
                value = shifted(value, cx, entry, entry)
            other = (YM if cy == 1 else YP).index(OPPOSITE[i]) * TOP
            back = faces[mine, other : other + TOP, :]
            usable = open_from[cx]
            if cz:
                value = roll(value, cz, 0)
                usable = usable & (sub != (0 if cz == 1 else TOP - 1))
            sums = add_to(sums, i, jnp.where(usable, value, back))
        density, momentum = sums
        for k in range(3):
            speed = jnp.where(is_fluid, momentum[k] / density, 0.0)
            for level in range(TOP):
                vel[2 + level // layers, k * layers + level % layers, row : row + 1, :] = speed[
                    level : level + 1
                ]


def flow_kernel(post, ysh, pops, cells, xl, xr, yu, yd, out, ext):
    is_fluid = own_fluid(cells) > 0.5
    out[:, 0:BASE] = pops[:, 0:BASE]

    def visit(level, i, pulled):
        out[i, BASE + level] = jnp.where(is_fluid, pulled, pops[i, BASE + level])

    pull(post, ysh, cells, xl, xr, ext, visit, yu, yd)


def gather_kernel(shards, adj, xl, xr, yu, yd, gu, gd, pulled, mean, diff):
    layers, rows, cols = adj.shape[1:]
    gz = lax.axis_index("gz")
    sub = iota((rows, cols), 0)
    below = jnp.where(gz == 0, 0.0, yu[HEAT_ROW : HEAT_ROW + rows, :])
    above = jnp.where(gz == shards - 1, 0.0, yd[HEAT_ROW : HEAT_ROW + rows, :])
    for z in range(layers):
        p = [adj[0, z]]
        at = (HEAT_LANE + z, HEAT_LANE + layers + z)
        edge = jnp.concatenate([roll(xr[...], LANES - 1 - lane) for lane in at], axis=0)
        p.append(shifted(adj[1, z], -1, None, edge))
        edge = jnp.concatenate([roll(xl[...], -lane) for lane in at], axis=0)
        p.append(shifted(adj[2, z], 1, edge, None))
        halo = jnp.broadcast_to(gd[z : z + 1, :], (rows, cols))
        p.append(jnp.where(sub == rows - 1, halo, roll(adj[3, z], -1, 0)))
        halo = jnp.broadcast_to(gu[z : z + 1, :], (rows, cols))
        p.append(jnp.where(sub == 0, halo, roll(adj[4, z], 1, 0)))
        p.append(adj[5, z + 1] if z + 1 < layers else above)
        p.append(adj[6, z - 1] if z > 0 else below)
        for j in range(7):
            pulled[j, z] = p[j]
        mean[z] = WEIGHT7[0] * p[0] + WEIGHT7[1] * (p[1] + p[2] + p[3] + p[4] + p[5] + p[6])
        for k in range(3):
            diff[k, z] = (4.0 * WEIGHT7[1]) * (p[2 * k + 1] - p[2 * k + 2])


def thermal_kernel(shards, pulled, mean, diff, va, out, wide):
    layers, _, _ = mean.shape
    gz = lax.axis_index("gz")
    srcs, planes, part = va.shape[:3]
    for q in range(planes):
        for s in range(srcs):
            wide[q, part * s : part * (s + 1), :] = va[s, q]
    mark = wide[planes - 1]
    is_fluid = (mark * jnp.where(gz >= shards // 2, 1.0, 0.0)) > 0.5
    heated = mark * jnp.where(gz == 0, 1.0, 0.0)
    omega = jnp.where(is_fluid, OMEGA_FLUID, OMEGA_SOLID)
    keep = 1.0 - omega
    for z in range(layers):
        dot = sum(wide[k * layers + z] * diff[k, z] for k in range(3))
        common = omega * (mean[z] + dot)
        if z == 0:
            common = common + heated
        for j in range(7):
            out[j, z] = keep * pulled[j, z] + common


def per_device(populations, cell_type, adjoint, sizes):
    nx, ny, nz = sizes
    axes = ("gx", "gy", "gz")

    def along(delta_x, delta_y):
        moves = []
        for a in range(nx):
            for b in range(ny * nz):
                a2, b2 = a + delta_x, b + delta_y
                if 0 <= a2 < nx and 0 <= b2 < ny * nz:
                    moves.append((a * ny * nz + b, a2 * ny * nz + b2))
        return moves

    def across(delta):
        moves = []
        for a in range(nx):
            for b in range(ny):
                for c in range(nz):
                    if 0 <= b + delta < ny:
                        moves.append(((a * ny + b) * nz + c, (a * ny + b + delta) * nz + c))
        return moves

    _, rows, cols = cell_type.shape
    layers, heat_rows = adjoint.shape[1:3]
    post, ysh, xp, xm, yp, ym, gp, gm, own_faces = pl.pallas_call(
        collide_kernel,
        out_shape=(
            f32(19, TOP, rows, cols),
            f32(10, TOP, rows, cols),
            f32(heat_rows // 2, LANES),
            f32(heat_rows // 2, LANES),
            f32(Y_ROWS, cols),
            f32(Y_ROWS, cols),
            f32(layers, cols),
            f32(layers, cols),
            f32(2, HEAT_ROW, cols),
        ),
        in_specs=[pl.BlockSpec(memory_space=pltpu.HBM)] * 3,
        out_specs=(VMEM,) * 9,
        scratch_shapes=[
            pltpu.VMEM((19, TOP, rows, cols), jnp.float32),
            pltpu.VMEM((1, rows, cols), jnp.int32),
            pltpu.VMEM(adjoint.shape, jnp.float32),
            pltpu.SemaphoreType.DMA((4,)),
        ],
        compiler_params=pltpu.CompilerParams(vmem_limit_bytes=16 << 20),
        name="collide",
    )(*(pltpu.with_memory_space_constraint(a, pltpu.HBM) for a in (populations, cell_type, adjoint)))
    xl = lax.ppermute(xp, axes, along(1, 0))
    xr = lax.ppermute(xm, axes, along(-1, 0))
    gu = lax.ppermute(gp, axes, across(1))
    gd = lax.ppermute(gm, axes, across(-1))
    top = jnp.concatenate([xl[rows - 1 : rows], xr[rows - 1 : rows]], axis=1)
    bottom = jnp.concatenate([xl[0:1], xr[0:1]], axis=1)
    yp = lax.dynamic_update_slice(yp, top, (CORNER_ROW, 0))
    ym = lax.dynamic_update_slice(ym, bottom, (CORNER_ROW, 0))
    yu = lax.ppermute(yp, axes, along(0, 1))
    yd = lax.ppermute(ym, axes, along(0, -1))
    small = pltpu.CompilerParams(vmem_limit_bytes=16 << 20)
    ext = pltpu.VMEM((2, 8, LANES), jnp.float32)
    vel, edge = pl.pallas_call(
        inner_velocity_kernel,
        out_shape=(f32(nz, 3 * layers + 1, rows, cols), f32(2, 4, TOP, cols)),
        in_specs=[VMEM] * 5,
        out_specs=(VMEM,) * 2,
        scratch_shapes=[ext],
        compiler_params=small,
        name="inner",
    )(post, ysh, cell_type, xl, xr)
    vel = pl.pallas_call(
        edge_velocity_kernel,
        out_shape=f32(*vel.shape),
        in_specs=[VMEM] * 6,
        out_specs=VMEM,
        compiler_params=small,
        name="edge",
    )(vel, edge, cell_type, own_faces, yu, yd)
    va = lax.all_to_all(vel, "gz", split_axis=0, concat_axis=0, tiled=True)
    flow_next = pl.pallas_call(
        flow_kernel,
        out_shape=f32(*populations.shape),
        in_specs=[VMEM] * 8,
        out_specs=VMEM,
        scratch_shapes=[ext],
        compiler_params=small,
        name="flow",
    )(post, ysh, populations, cell_type, xl, xr, yu, yd)
    pulled, mean, diff = pl.pallas_call(
        functools.partial(gather_kernel, nz),
        out_shape=(f32(*adjoint.shape), f32(layers, heat_rows, cols), f32(3, layers, heat_rows, cols)),
        in_specs=[VMEM] * 7,
        out_specs=(VMEM,) * 3,
        compiler_params=small,
        name="gather",
    )(adjoint, xl, xr, yu, yd, gu, gd)
    adjoint_prev = pl.pallas_call(
        functools.partial(thermal_kernel, nz),
        out_shape=f32(*adjoint.shape),
        in_specs=[VMEM] * 4,
        out_specs=VMEM,
        scratch_shapes=[pltpu.VMEM((3 * layers + 1, heat_rows, cols), jnp.float32)],
        compiler_params=small,
        name="thermal",
    )(pulled, mean, diff, va)
    return flow_next, adjoint_prev


def solution(mesh):
    sizes = tuple(mesh.shape[axis] for axis in ("gx", "gy", "gz"))
    placed = (
        P(None, None, ("gy", "gz"), "gx"),
        P(None, ("gy", "gz"), "gx"),
        P(None, "gz", "gy", "gx"),
    )

    def body(p, c, a):
        return per_device(p, c, a, sizes)

    return jax.shard_map(
        body,
        mesh=mesh,
        in_specs=placed,
        out_specs=(P(None, None, ("gy", "gz"), "gx"), P(None, "gz", "gy", "gx")),
        check_vma=False,
    )
```

```python
import functools

import jax
import jax.numpy as jnp
from jax import lax
from jax.experimental import pallas as pl
from jax.experimental.pallas import tpu as pltpu
from jax.sharding import PartitionSpec as P


VEL19 = [
    (0, 0, 0),
    (1, 0, 0),
    (-1, 0, 0),
    (0, 1, 0),
    (0, -1, 0),
    (0, 0, 1),
    (0, 0, -1),
    (1, 1, 0),
    (-1, -1, 0),
    (1, -1, 0),
    (-1, 1, 0),
    (1, 0, 1),
    (-1, 0, -1),
    (1, 0, -1),
    (-1, 0, 1),
    (0, 1, 1),
    (0, -1, -1),
    (0, 1, -1),
    (0, -1, 1),
]
WEIGHT19 = [1.0 / 3.0] + [1.0 / 18.0] * 6 + [1.0 / 36.0] * 12
OPPOSITE = [0, 2, 1, 4, 3, 6, 5, 8, 7, 10, 9, 12, 11, 14, 13, 16, 15, 18, 17]
WEIGHT7 = [0.25] + [0.125] * 6
OMEGA_FLOW = 1.6
OMEGA_FLUID = 1.25
OMEGA_SOLID = 1.6

BASE = 8
TOP = 8
LANES = 128
XP = [1, 7, 9, 11, 13]
XM = [2, 8, 10, 12, 14]
YP = [3, 7, 10, 15, 17]
YM = [4, 8, 9, 18, 16]
YALL = YP + YM
FLAG_LANE = 40
HEAT_LANE = 64
FLAG_ROW = 31
CORNER_ROW = 32
HEAT_ROW = 40
CODE_ROW = 56
Y_ROWS = 64
CHUNKS = 1
VMEM = pl.BlockSpec(memory_space=pltpu.VMEM)
HBM = pl.BlockSpec(memory_space=pltpu.HBM)


def f32(*shape):
    return jax.ShapeDtypeStruct(shape, jnp.float32)


def iota(shape, axis):
    return lax.broadcasted_iota(jnp.int32, shape, axis)


def roll(value, shift, axis=1):
    size = value.shape[axis]
    shift = shift % size
    return value if shift == 0 else pltpu.roll(value, shift, axis)


def collide_kernel(
    pops_in, cells_in, adj_in, post, ysh, xp, xm, yp, ym, gp, gm, faces, codes, pops, cells, adj, sem
):
    rows, cols = cells.shape[1:]
    chunk = TOP // CHUNKS
    loads = [
        pltpu.make_async_copy(
            pops_in.at[:, BASE + k * chunk : BASE + (k + 1) * chunk],
            pops.at[:, k * chunk : (k + 1) * chunk],
            sem.at[k],
        )
        for k in range(CHUNKS)
    ]
    loads.append(pltpu.make_async_copy(cells_in.at[BASE], cells.at[0], sem.at[CHUNKS]))
    loads.append(pltpu.make_async_copy(adj_in.at[1:3], adj.at[1:3], sem.at[CHUNKS + 1]))
    loads.append(pltpu.make_async_copy(adj_in.at[3:7], adj.at[3:7], sem.at[CHUNKS + 2]))
    loads.append(pltpu.make_async_copy(cells_in.at[0], cells.at[1], sem.at[CHUNKS + 3]))
    for load in [loads[CHUNKS], loads[CHUNKS + 3]] + loads[:CHUNKS] + loads[CHUNKS + 1 : CHUNKS + 3]:
        load.start()
    loads[CHUNKS].wait()
    left, right = slice(0, LANES), slice(cols - LANES, cols)
    lane = iota((rows, LANES), 1)
    fluid = jnp.where(cells[0] == 0, 1.0, 0.0)
    to_right = jnp.where(lane == FLAG_LANE, roll(fluid[:, right], FLAG_LANE + 1), 0.0)
    to_left = jnp.where(lane == FLAG_LANE, roll(fluid[:, left], FLAG_LANE), 0.0)
    for level in range(TOP):
        if level % chunk == 0:
            loads[level // chunk].wait()
        f = [pops[i, level] for i in range(19)]
        density = sum(f[1:], f[0])
        u = []
        for k in range(3):
            plus = sum(f[i] for i in range(19) if VEL19[i][k] == 1)
            minus = sum(f[i] for i in range(19) if VEL19[i][k] == -1)
            u.append((plus - minus) / density)
        common = 1.0 - 1.5 * (u[0] * u[0] + u[1] * u[1] + u[2] * u[2])
        scaled = OMEGA_FLOW * density
        for i in range(19):
            c = VEL19[i]
            cu = None
            for k in range(3):
                if c[k]:
                    term = u[k] if c[k] == 1 else -u[k]
                    cu = term if cu is None else cu + term
            shape = common if cu is None else common + cu * (3.0 + 4.5 * cu)
            out = (1.0 - OMEGA_FLOW) * f[i] + (WEIGHT19[i] * scaled) * shape
            post[i, level] = out
            if i in XP:
                at = XP.index(i) * TOP + level
                to_right = jnp.where(lane == at, roll(out[:, right], at + 1), to_right)
            if i in XM:
                at = XM.index(i) * TOP + level
                to_left = jnp.where(lane == at, roll(out[:, left], at), to_left)
            if i in YP:
                at = YP.index(i) * TOP + level
                faces[0, at : at + 1, :] = out[rows - 1 : rows]
                ysh[YALL.index(i), level, 1:rows, :] = out[0 : rows - 1]
            if i in YM:
                at = YM.index(i) * TOP + level
                faces[1, at : at + 1, :] = out[0:1]
                ysh[YALL.index(i), level, 0 : rows - 1, :] = out[1:rows]
    loads[CHUNKS + 1].wait()
    loads[CHUNKS + 2].wait()
    loads[CHUNKS + 3].wait()
    code = jnp.where(cells[1] == 2, 1.0, 0.0)
    codes[...] = code
    ym[CODE_ROW : CODE_ROW + rows, :] = code
    layers, arows = adj.shape[1:3]
    packed = arows // 2
    heat_right = jnp.zeros((packed, LANES), jnp.float32)
    heat_left = heat_right
    lane = iota((packed, LANES), 1)
    for z in range(layers):
        for part in range(2):
            at = HEAT_LANE + part * layers + z
            block = slice(part * packed, (part + 1) * packed)
            heat_right = jnp.where(lane == at, roll(adj[2, z, block, right], at + 1), heat_right)
            heat_left = jnp.where(lane == at, roll(adj[1, z, block, left], at), heat_left)
        gp[z : z + 1, :] = adj[4, z, arows - 1 : arows, :]
        gm[z : z + 1, :] = adj[3, z, 0:1, :]
    xp[...] = heat_right
    xm[...] = heat_left
    lane = iota((rows, LANES), 1)
    xp[0:rows, :] = jnp.where(lane < HEAT_LANE, to_right, heat_right[0:rows])
    xm[0:rows, :] = jnp.where(lane < HEAT_LANE, to_left, heat_left[0:rows])
    yp[0:HEAT_ROW, :] = faces[0]
    ym[0:HEAT_ROW, :] = faces[1]
    yp[FLAG_ROW : FLAG_ROW + 1, :] = fluid[rows - 1 : rows]
    ym[FLAG_ROW : FLAG_ROW + 1, :] = fluid[0:1]
    yp[HEAT_ROW : HEAT_ROW + arows, :] = adj[6, layers - 1]
    ym[HEAT_ROW : HEAT_ROW + arows, :] = adj[5, 0]


def own_fluid(cells):
    return jnp.where(cells[BASE] == 0, 1.0, 0.0)


def shifted(value, cx, left, right):
    if cx == 0:
        return value
    col = iota((value.shape[0], LANES), 1)
    value = roll(value, cx)
    if cx == 1:
        patched = jnp.where(col == 0, left, value[:, 0:LANES])
        return jnp.concatenate([patched, value[:, LANES:]], axis=1)
    last = value.shape[1] - LANES
    patched = jnp.where(col == LANES - 1, right, value[:, last:])
    return jnp.concatenate([value[:, 0:last], patched], axis=1)


def columns_beyond(ext, xl, xr, rows, yu=None, yd=None):
    zero = jnp.zeros((1, LANES), jnp.float32)
    for side, own in ((0, xl), (1, xr)):
        part = slice(side * LANES, (side + 1) * LANES)
        ext[side, 0:1, :] = zero if yu is None else yu[CORNER_ROW : CORNER_ROW + 1, part]
        ext[side, 1 : rows + 1, :] = own[0:rows, :]
        ext[side, rows + 1 : rows + 2, :] = zero if yd is None else yd[CORNER_ROW : CORNER_ROW + 1, part]
    return {
        (side, cy): ext[side, 1 - cy : 1 - cy + rows, :] for side in (0, 1) for cy in (-1, 0, 1)
    }


def pull(post, ysh, cells, xl, xr, ext, visit, yu=None, yd=None):
    rows, cols = cells.shape[1:]
    sub = iota((rows, cols), 0)
    beyond = columns_beyond(ext, xl, xr, rows, yu, yd)

    def shift_x(value, cx, cy, lane_at):
        if cx == 1:
            return shifted(value, 1, roll(beyond[0, cy], -lane_at), None)
        if cx == -1:
            return shifted(value, -1, None, roll(beyond[1, cy], LANES - 1 - lane_at))
        return value

    def halo_row(value, cy, at):
        if cy == 0 or yu is None:
            return value
        halo = jnp.broadcast_to((yu if cy == 1 else yd)[at : at + 1, :], (rows, cols))
        return jnp.where(sub == (0 if cy == 1 else rows - 1), halo, value)

    fluid = own_fluid(cells)
    spread = {
        0: fluid,
        1: halo_row(jnp.concatenate([fluid[rows - 1 : rows], fluid[0 : rows - 1]], axis=0), 1, FLAG_ROW),
        -1: halo_row(jnp.concatenate([fluid[1:rows], fluid[0:1]], axis=0), -1, FLAG_ROW),
    }
    open_from = {
        (cx, cy): shift_x(spread[cy], cx, cy, FLAG_LANE) > 0.5
        for cx in (-1, 0, 1)
        for cy in (-1, 0, 1)
    }
    for level in range(TOP):
        for i in range(19):
            cx, cy, cz = VEL19[i]
            back = post[OPPOSITE[i], level]
            source = level - cz
            if i == 0 or source < 0 or source >= TOP:
                visit(level, i, back)
                continue
            if cy == 0:
                value = post[i, source]
            else:
                at = (YP if cy == 1 else YM).index(i) * TOP + source
                value = halo_row(ysh[YALL.index(i), source], cy, at)
            if cx:
                value = shift_x(value, cx, cy, (XP if cx == 1 else XM).index(i) * TOP + source)
            visit(level, i, jnp.where(open_from[cx, cy], value, back))


def add_to(sums, i, value):
    density, momentum = sums
    density = value if density is None else density + value
    momentum = list(momentum)
    for k in range(3):
        c = VEL19[i][k]
        if c:
            term = value if c == 1 else -value
            momentum[k] = term if momentum[k] is None else momentum[k] + term
    return density, momentum


def inner_velocity_kernel(post, ysh, cells, xl, xr, vel, edge, ext):
    rows, cols = cells.shape[1:]
    sub = iota((rows, cols), 0)
    is_fluid = own_fluid(cells) > 0.5
    layers = vel.shape[1] // 3
    state = {}

    def visit(level, i, pulled):
        cy = VEL19[i][1]
        if cy:
            pulled = jnp.where(sub == (0 if cy == 1 else rows - 1), 0.0, pulled)
        sums = add_to(state.get(level, (None, [None] * 3)), i, pulled)
        state[level] = sums
        if i == 18:
            density, momentum = sums
            for k, part in enumerate([density] + momentum):
                edge[0, k, level : level + 1, :] = part[0:1]
                edge[1, k, level : level + 1, :] = part[rows - 1 : rows]
            for k in range(3):
                vel[level // layers, k * layers + level % layers] = jnp.where(
                    is_fluid, momentum[k] / density, 0.0
                )

    pull(post, ysh, cells, xl, xr, ext, visit)


def edge_velocity_kernel(vel_in, edge, cells, faces, yu, yd, codes, pa, pb, pc, own, near, vel):
    rows, cols = cells.shape[1:]
    layers = vel.shape[1] // 3
    gz = lax.axis_index("gz")
    sub = iota((TOP, cols), 0)
    fluid = own_fluid(cells)
    vel[...] = vel_in[...]
    for side, (row, cy, pops, source, mine) in enumerate(
        ((0, 1, YP, yu, 1), (rows - 1, -1, YM, yd, 0))
    ):
        is_fluid = jnp.broadcast_to(fluid[row : row + 1], (TOP, cols)) > 0.5
        corner = [
            jnp.broadcast_to(source[CORNER_ROW : CORNER_ROW + 1, part], (TOP, LANES))
            for part in (slice(0, LANES), slice(LANES, 2 * LANES))
        ]
        flags = jnp.broadcast_to(source[FLAG_ROW : FLAG_ROW + 1, :], (TOP, cols))
        open_from = {
            0: flags > 0.5,
            1: shifted(flags, 1, roll(corner[0], -FLAG_LANE), None) > 0.5,
            -1: shifted(flags, -1, None, roll(corner[1], LANES - 1 - FLAG_LANE)) > 0.5,
        }
        sums = (edge[side, 0], [edge[side, 1], edge[side, 2], edge[side, 3]])
        for at, i in enumerate(pops):
            cx, _, cz = VEL19[i]
            value = source[at * TOP : (at + 1) * TOP, :]
            if cx:
                first = (XP if cx == 1 else XM).index(i) * TOP
                column = corner[0 if cx == 1 else 1]
                entry = jnp.zeros((TOP, LANES), jnp.float32)
                goal = 0 if cx == 1 else LANES - 1
                level_of = iota((TOP, LANES), 0)
                for level in range(TOP):
                    entry = jnp.where(level_of == level, roll(column, goal - first - level), entry)
                value = shifted(value, cx, entry, entry)
            other = (YM if cy == 1 else YP).index(OPPOSITE[i]) * TOP
            back = faces[mine, other : other + TOP, :]
            usable = open_from[cx]
            if cz:
                value = roll(value, cz, 0)
                usable = usable & (sub != (0 if cz == 1 else TOP - 1))
            sums = add_to(sums, i, jnp.where(usable, value, back))
        density, momentum = sums
        for k in range(3):
            speed = jnp.where(is_fluid, momentum[k] / density, 0.0)
            for level in range(TOP):
                vel[level // layers, k * layers + level % layers, row : row + 1, :] = speed[
                    level : level + 1
                ]
    for buffer, lower in ((pa, 1), (pb, 0), (pc, 3), (own, 2)):
        buffer[0 : 3 * layers] = vel[jnp.where(gz == lower, 0, 1)]
    pa[3 * layers] = fluid
    pb[3 * layers] = fluid
    pc[3 * layers] = fluid
    near[0] = codes[...]
    near[1] = yd[CODE_ROW : CODE_ROW + rows, :]
    own[3 * layers] = jnp.where(gz == 0, codes[...], fluid)


def flow_kernel(post, ysh, pops, cells, xl, xr, yu, yd, out, ext):
    is_fluid = own_fluid(cells) > 0.5
    out[:, 0:BASE] = pops[:, 0:BASE]

    def visit(level, i, pulled):
        out[i, BASE + level] = jnp.where(is_fluid, pulled, pops[i, BASE + level])

    pull(post, ysh, cells, xl, xr, ext, visit, yu, yd)


def gather_kernel(shards, adj, xl, xr, yu, yd, gu, gd, pulled, mean, diff):
    layers, rows, cols = adj.shape[1:]
    gz = lax.axis_index("gz")
    sub = iota((rows, cols), 0)
    below = jnp.where(gz == 0, 0.0, yu[HEAT_ROW : HEAT_ROW + rows, :])
    above = jnp.where(gz == shards - 1, 0.0, yd[HEAT_ROW : HEAT_ROW + rows, :])
    for z in range(layers):
        p = [adj[0, z]]
        at = (HEAT_LANE + z, HEAT_LANE + layers + z)
        edge = jnp.concatenate([roll(xr[...], LANES - 1 - lane) for lane in at], axis=0)
        p.append(shifted(adj[1, z], -1, None, edge))
        edge = jnp.concatenate([roll(xl[...], -lane) for lane in at], axis=0)
        p.append(shifted(adj[2, z], 1, edge, None))
        halo = jnp.broadcast_to(gd[z : z + 1, :], (rows, cols))
        p.append(jnp.where(sub == rows - 1, halo, roll(adj[3, z], -1, 0)))
        halo = jnp.broadcast_to(gu[z : z + 1, :], (rows, cols))
        p.append(jnp.where(sub == 0, halo, roll(adj[4, z], 1, 0)))
        p.append(adj[5, z + 1] if z + 1 < layers else above)
        p.append(adj[6, z - 1] if z > 0 else below)
        for j in range(7):
            pulled[j, z] = p[j]
        mean[z] = WEIGHT7[0] * p[0] + WEIGHT7[1] * (p[1] + p[2] + p[3] + p[4] + p[5] + p[6])
        for k in range(3):
            diff[k, z] = (4.0 * WEIGHT7[1]) * (p[2 * k + 1] - p[2 * k + 2])


def thermal_kernel(pulled, mean, diff, pa, pb, pc, own, near, far, result, wide, out, sem):
    layers, _, _ = mean.shape
    gz = lax.axis_index("gz")
    planes, part = own.shape[:2]
    at_two, at_zero = gz == 2, gz == 0
    for q in range(planes):
        a, b, c, mine = pa[q], pb[q], pc[q], own[q]
        blocks = [
            jnp.where(at_two, b, a),
            jnp.where(at_two, a, b),
            jnp.where(at_two, mine, c),
            jnp.where(at_two, c, mine),
        ]
        if q == planes - 1:
            heat = (mine, near[0], near[1], far[...])
            blocks = [jnp.where(at_zero, v, w) for v, w in zip(heat, blocks)]
        for s in range(4):
            wide[q, part * s : part * (s + 1), :] = blocks[s]
    mark = wide[planes - 1]
    is_fluid = (mark * jnp.where(gz >= 2, 1.0, 0.0)) > 0.5
    heated = mark * jnp.where(at_zero, 1.0, 0.0)
    omega = jnp.where(is_fluid, OMEGA_FLUID, OMEGA_SOLID)
    keep = 1.0 - omega
    for z in range(layers):
        dot = sum(wide[k * layers + z] * diff[k, z] for k in range(3))
        common = omega * (mean[z] + jnp.where(is_fluid, dot, 0.0))
        if z == 0:
            common = common + heated
        for j in range(7):
            out[j, z] = keep * pulled[j, z] + common
        pltpu.make_async_copy(out.at[:, z], result.at[:, z], sem.at[z]).start()
    for z in range(layers):
        pltpu.make_async_copy(out.at[:, z], result.at[:, z], sem.at[z]).wait()


def per_device(populations, cell_type, adjoint, sizes):
    nx, ny, nz = sizes
    axes = ("gx", "gy", "gz")

    def along(delta_x, delta_y):
        moves = []
        for a in range(nx):
            for b in range(ny * nz):
                a2, b2 = a + delta_x, b + delta_y
                if 0 <= a2 < nx and 0 <= b2 < ny * nz:
                    moves.append((a * ny * nz + b, a2 * ny * nz + b2))
        return moves

    def across(delta):
        moves = []
        for a in range(nx):
            for b in range(ny):
                for c in range(nz):
                    if 0 <= b + delta < ny:
                        moves.append(((a * ny + b) * nz + c, (a * ny + b + delta) * nz + c))
        return moves

    def move_inside(value, pairs):
        moves = [(g * nz + i, g * nz + j) for g in range(nx * ny) for i, j in pairs]
        return lax.ppermute(value, axes, moves)

    _, rows, cols = cell_type.shape
    layers, heat_rows = adjoint.shape[1:3]
    post, ysh, xp, xm, yp, ym, gp, gm, own_faces, codes = pl.pallas_call(
        collide_kernel,
        out_shape=(
            f32(19, TOP, rows, cols),
            f32(10, TOP, rows, cols),
            f32(heat_rows // 2, LANES),
            f32(heat_rows // 2, LANES),
            f32(Y_ROWS, cols),
            f32(Y_ROWS, cols),
            f32(layers, cols),
            f32(layers, cols),
            f32(2, HEAT_ROW, cols),
            f32(rows, cols),
        ),
        in_specs=[pl.BlockSpec(memory_space=pltpu.HBM)] * 3,
        out_specs=(VMEM,) * 10,
        scratch_shapes=[
            pltpu.VMEM((19, TOP, rows, cols), jnp.float32),
            pltpu.VMEM((2, rows, cols), jnp.int32),
            pltpu.VMEM(adjoint.shape, jnp.float32),
            pltpu.SemaphoreType.DMA((CHUNKS + 4,)),
        ],
        compiler_params=pltpu.CompilerParams(vmem_limit_bytes=16 << 20),
        name="collide",
    )(*(pltpu.with_memory_space_constraint(a, pltpu.HBM) for a in (populations, cell_type, adjoint)))
    xl = lax.ppermute(xp, axes, along(1, 0))
    xr = lax.ppermute(xm, axes, along(-1, 0))
    gu = lax.ppermute(gp, axes, across(1))
    gd = lax.ppermute(gm, axes, across(-1))
    far = move_inside(codes, ((3, 0),))
    top = jnp.concatenate([xl[rows - 1 : rows], xr[rows - 1 : rows]], axis=1)
    bottom = jnp.concatenate([xl[0:1], xr[0:1]], axis=1)
    yp = lax.dynamic_update_slice(yp, top, (CORNER_ROW, 0))
    ym = lax.dynamic_update_slice(ym, bottom, (CORNER_ROW, 0))
    yu = lax.ppermute(yp, axes, along(0, 1))
    yd = lax.ppermute(ym, axes, along(0, -1))
    small = pltpu.CompilerParams(vmem_limit_bytes=16 << 20)
    ext = pltpu.VMEM((2, 8, LANES), jnp.float32)
    vel, edge = pl.pallas_call(
        inner_velocity_kernel,
        out_shape=(f32(2, 3 * layers, rows, cols), f32(2, 4, TOP, cols)),
        in_specs=[VMEM] * 5,
        out_specs=(VMEM,) * 2,
        scratch_shapes=[ext],
        compiler_params=small,
        name="inner",
    )(post, ysh, cell_type, xl, xr)
    planes = f32(3 * layers + 1, rows, cols)
    pa, pb, pc, own, near = pl.pallas_call(
        edge_velocity_kernel,
        out_shape=(planes,) * 4 + (f32(2, rows, cols),),
        in_specs=[VMEM] * 7,
        out_specs=(VMEM,) * 5,
        scratch_shapes=[pltpu.VMEM((2, 3 * layers, rows, cols), jnp.float32)],
        compiler_params=small,
        name="edge",
    )(vel, edge, cell_type, own_faces, yu, yd, codes)
    near = move_inside(near, ((1, 0),))
    pa = move_inside(pa, ((1, 2), (0, 3)))
    pb = move_inside(pb, ((0, 2), (1, 3)))
    pc = move_inside(pc, ((2, 3), (3, 2)))
    flow_next = pl.pallas_call(
        flow_kernel,
        out_shape=f32(*populations.shape),
        in_specs=[VMEM] * 8,
        out_specs=VMEM,
        scratch_shapes=[ext],
        compiler_params=small,
        name="flow",
    )(post, ysh, populations, cell_type, xl, xr, yu, yd)
    pulled, mean, diff = pl.pallas_call(
        functools.partial(gather_kernel, nz),
        out_shape=(f32(*adjoint.shape), f32(layers, heat_rows, cols), f32(3, layers, heat_rows, cols)),
        in_specs=[VMEM] * 7,
        out_specs=(VMEM,) * 3,
        compiler_params=small,
        name="gather",
    )(adjoint, xl, xr, yu, yd, gu, gd)
    adjoint_prev = pl.pallas_call(
        thermal_kernel,
        out_shape=f32(*adjoint.shape),
        in_specs=[VMEM] * 9,
        out_specs=HBM,
        scratch_shapes=[
            pltpu.VMEM((3 * layers + 1, heat_rows, cols), jnp.float32),
            pltpu.VMEM(adjoint.shape, jnp.float32),
            pltpu.SemaphoreType.DMA((layers,)),
        ],
        compiler_params=small,
        name="thermal",
    )(pulled, mean, diff, pa, pb, pc, own, near, far)
    return flow_next, adjoint_prev


def solution(mesh):
    sizes = tuple(mesh.shape[axis] for axis in ("gx", "gy", "gz"))
    placed = (
        P(None, None, ("gy", "gz"), "gx"),
        P(None, ("gy", "gz"), "gx"),
        P(None, "gz", "gy", "gx"),
    )

    def body(p, c, a):
        return per_device(p, c, a, sizes)

    return jax.shard_map(
        body,
        mesh=mesh,
        in_specs=placed,
        out_specs=(P(None, None, ("gy", "gz"), "gx"), P(None, "gz", "gy", "gx")),
        check_vma=False,
    )
```
